512 devices in a mesh: ctx: 64 (over x, z), fsdp: 8 (over y, core).
Axes of the slice: x: 4, y: 4, z: 16, core: 2. Of those that a mesh axis runs over, the one named last changes fastest.
Arguments:
- tokens: bfloat16 [8, 8192, 4096], P('fsdp', 'ctx'), may hold values from -6 to 6
- queries: bfloat16 [8, 8192, 512], P('fsdp', 'ctx'), may hold values from -6 to 6
- flags: int32 [8, 8192], P('fsdp', 'ctx'), may hold values from 0 to 1, as said below
- w_key: bfloat16 [4096, 512], P(('ctx', 'fsdp')), may hold values from -0.09375 to 0.09375
- w_value: bfloat16 [4096, 512], P(('ctx', 'fsdp')), may hold values from -0.09375 to 0.09375
- norm_gain: float32 [512], replicated, may hold values from 0.25 to 1.75
Outputs:
- attended: bfloat16 [8, 8192, 512], P('fsdp', 'ctx')
The draws below stay inside these ranges and needn't reach their ends.
Inputs may be any that keep to these rules, and one draw needn't show every extreme that they name: `flags`: in each sequence a document starts at token 0 and at every token k * 2048 + 2048 // 2; other tokens start one at random, never before token 3072 and never at the first token of a block. No document is longer than 2048 tokens.
All inputs are finite; a program needn't handle non-finite values.
Results may differ from the reference program's by a relative error of at most 0.0053.
Values may be sent and summed in bfloat16 or wider, within the bound.
A program may use at most 64 MiB of HBM per device.

```python
import jax
import jax.numpy as jnp
from jax import lax

D = 4096
HEAD = 128
HEADS = 4
TOK_DEV = 128
HD = 512
DOC_MOST = 2048
LEN = 8192
SEQS = 8
N_CTX = 64


def draw_flags(key, part):
    places = jnp.arange(LEN, dtype=jnp.int32)
    half_doc = DOC_MOST // 2
    forced = (places == 0) | (places % DOC_MOST == half_doc)
    picks = jax.random.randint(key, (SEQS, LEN), 0, 4 * TOK_DEV)
    allowed = (places >= DOC_MOST + half_doc) & (places % TOK_DEV != 0)
    extra = (picks == 0) & allowed[None, :]
    return (forced[None, :] | extra).astype(jnp.int32)


def shard_levels(rng, shape, pieces, least, largest):
    level, own = 1.0, jax.random.fold_in(rng, 6)
    for dim, blocks in pieces:
        steps = jnp.exp(jax.random.uniform(jax.random.fold_in(own, dim), (blocks,), jnp.float32, least / len(pieces), largest / len(pieces)))
        level = level * jnp.repeat(steps, shape[dim] // blocks).reshape([-1 if axis == dim else 1 for axis in range(len(shape))])
    return level


def gaussian(rng, dims, spread, bound, cuts=(), kind=jnp.bfloat16):
    values = jax.random.normal(rng, dims, jnp.float32) * spread
    if len(cuts) > 0:
        values = shard_levels(rng, dims, cuts, -0.22, 0.18) * values
    return jnp.clip(values, min=-bound, max=bound).astype(kind)


def setup_inputs(seed: int = 0) -> dict:
    keys = jax.random.split(jax.random.key(seed), 7)
    return {
        "tokens": gaussian(keys[0], (SEQS, LEN, D), 1.0, 6.0, ((0, 8), (1, 64))),
        "queries": gaussian(keys[1], (SEQS, LEN, HD), 1.0, 6.0, ((0, 8), (1, 64))),
        "flags": draw_flags(jax.random.fold_in(keys[6], 71), 0),
        "w_key": gaussian(keys[3], (D, HD), D ** -0.5, 0.09375, ((0, 512),)),
        "w_value": gaussian(keys[4], (D, HD), D ** -0.5, 0.09375, ((0, 512),)),
        "norm_gain": jnp.clip(1.0 + 0.15 * jax.random.normal(keys[5], (HD,), jnp.float32), 0.25, 1.75),
    }


def feature(u):
    return jax.nn.elu(u) + 1.0

def block_step(norm_gain, carried, item):
    query, key, value, marks = item
    seg = jnp.cumsum(marks).astype(jnp.int32)
    last = seg[TOK_DEV - 1]
    reset = (last > 0).astype(jnp.float32)
    tail = (seg == last).astype(key.dtype)
    local_state = jnp.einsum('the,thf->hef', (key * tail[:, None, None]).astype(jnp.float32), value.astype(jnp.float32))
    carried_b = carried.astype(jnp.bfloat16)
    first = (seg == 0).astype(jnp.float32)
    carried_term = jnp.einsum('the,hef->thf', query.astype(jnp.float32), carried_b.astype(jnp.float32)) * first[:, None, None]
    places = jnp.arange(TOK_DEV, dtype=jnp.int32)
    allowed = (places[None, :] <= places[:, None]) & (seg[None, :] == seg[:, None])
    scores = jnp.einsum('the,she->hts', query.astype(jnp.float32), key.astype(jnp.float32))
    scores = jnp.where(allowed[None, :, :], scores, 0.0).astype(jnp.bfloat16)
    inside = jnp.einsum('hts,shf->thf', scores.astype(jnp.float32), value.astype(jnp.float32))
    mixed = carried_term + inside
    scale = lax.rsqrt(lax.optimization_barrier(jnp.mean(mixed * mixed, axis=-1, keepdims=True)) + 1e-06)
    attended = (mixed * scale * norm_gain.reshape(HEADS, HEAD)).astype(jnp.bfloat16)
    new_carried = (1.0 - reset) * carried + local_state
    return (new_carried, attended)

def reference(tokens, queries, flags, w_key, w_value, norm_gain):
    results = []
    for seq in range(SEQS):
        key = feature(jnp.dot(tokens[seq], w_key, preferred_element_type=jnp.float32)).astype(jnp.bfloat16)
        value = jnp.dot(tokens[seq], w_value, preferred_element_type=jnp.float32).astype(jnp.bfloat16)
        query = feature(queries[seq].astype(jnp.float32)).astype(jnp.bfloat16)
        key = key.reshape(N_CTX, TOK_DEV, HEADS, HEAD)
        value = value.reshape(N_CTX, TOK_DEV, HEADS, HEAD)
        query = query.reshape(N_CTX, TOK_DEV, HEADS, HEAD)
        marks = flags[seq].reshape(N_CTX, TOK_DEV)
        start = jnp.zeros((HEADS, HEAD, HEAD), jnp.float32)
        final, blocks = lax.scan(lambda c, it: block_step(norm_gain, c, it), start, (query, key, value, marks))
        results.append(blocks.reshape(LEN, HD))
    return jnp.stack(results)
```

```python
import functools

import jax
import jax.numpy as jnp
from jax import lax
from jax.experimental import pallas as pl
from jax.experimental.pallas import tpu as pltpu
from jax.sharding import PartitionSpec as P

HEAD = 128
MESH = pl.DeviceIdType.MESH
NX, NY, NZ = 4, 4, 16
GROUP = 16
F32, BF16 = jnp.float32, jnp.bfloat16


def device(x, z, y, c):
    return (x * NZ + z, y * 2 + c)


def phi(u):
    return jnp.where(u > 0, u + 1.0, jnp.exp(jnp.minimum(u, 0.0)))


def segments(marks):
    n = marks.shape[1]
    t = lax.broadcasted_iota(jnp.int32, (n, n), 0)
    s = lax.broadcasted_iota(jnp.int32, (n, n), 1)
    wide = jnp.broadcast_to(marks, (n, n)).astype(F32)
    column = jnp.sum(jnp.where(s <= t, wide, 0.0), axis=1, keepdims=True)
    upright = jnp.sum(jnp.where(s == t, wide, 0.0), axis=1, keepdims=True)
    row = jnp.sum(jnp.where(t <= s, jnp.broadcast_to(upright, (n, n)), 0.0), axis=0, keepdims=True)
    last = jnp.sum(marks.astype(F32), axis=1, keepdims=True)
    return column, row, last


def kernel(
    tok, qry, flg, wk, wv, gain, out,
    T, Q, F, WB, W, acc, KV, KB, KR, ST, SR, CS, CR, MIX,
    loc, pair_s, pair_r, z_s, z_r, two_s, two_r, three_s, three_r, k_s, k_r, s1_s, s1_r, s2_s, s2_r,
):
    ctx, fsdp = lax.axis_index("ctx"), lax.axis_index("fsdp")
    x, z = ctx // NZ, lax.rem(ctx, NZ)
    y, c = fsdp // 2, lax.rem(fsdp, 2)
    other = 1 - c
    sibling = device(x, z, y, other)

    loads = [
        pltpu.make_async_copy(wk, WB.at[c, 0], loc.at[0]),
        pltpu.make_async_copy(wv, WB.at[c, 1], loc.at[1]),
        pltpu.make_async_copy(flg, F.at[c], loc.at[2]),
        pltpu.make_async_copy(tok, T.at[c], loc.at[3]),
        pltpu.make_async_copy(qry, Q, loc.at[4]),
    ]
    for load in loads:
        load.start()

    barrier = pltpu.get_barrier_semaphore()

    def greet(to):
        pl.semaphore_signal(barrier, inc=1, device_id=to, device_id_type=MESH)

    def greet_z(d, carry):
        greet(device(x, lax.rem(z + d, NZ), y, c))
        return carry

    lax.fori_loop(1, NZ, greet_z, 0)
    for d in range(1, 4):
        greet(device(lax.rem(x + d, NX), z, y, c))
        greet(device(x, z, lax.rem(y + d, NY), c))
    greet(sibling)
    for load in loads[:3]:
        load.wait()
    pl.semaphore_wait(barrier, 22)

    def send(src, dst, ss, rs, to):
        return pltpu.make_async_remote_copy(
            src_ref=src, dst_ref=dst, send_sem=ss, recv_sem=rs, device_id=to, device_id_type=MESH
        )

    swap_w = send(WB.at[c], WB.at[c], pair_s.at[0], pair_r.at[0], sibling)
    swap_f = send(F.at[c], F.at[c], pair_s.at[1], pair_r.at[1], sibling)
    swap_w.start()
    swap_f.start()
    swap_w.wait()
    both = jnp.concatenate([WB[0].astype(F32), WB[1].astype(F32)], axis=1)
    low, high = both[:, :, : 2 * HEAD], both[:, :, 2 * HEAD :]
    mine = jnp.where(c == 0, low, high).astype(BF16)
    for h in range(2):
        cut = slice(h * HEAD, (h + 1) * HEAD)
        W[h, x, z, y] = jnp.concatenate([mine[0, :, cut], mine[1, :, cut]], axis=1)

    def z_copy(d):
        piece = W.at[:, x, z, y]
        return send(piece, piece, z_s.at[d], z_r.at[d], device(x, lax.rem(z + d, NZ), y, c))

    def z_start(d, carry):
        z_copy(d).start()
        return carry

    def z_wait(d, carry):
        z_copy(d).wait()
        return carry

    lax.fori_loop(1, NZ, z_start, 0)
    loads[3].wait()
    swap_t = send(T.at[c], T.at[c], pair_s.at[2], pair_r.at[2], sibling)
    swap_t.start()
    swap_f.wait()
    lax.fori_loop(1, NZ, z_wait, 0)

    def two(d):
        a, b = W.at[0, x, :, y], W.at[1, x, :, y]
        return (
            send(a, a, two_s.at[0, d], two_r.at[0, d], device(x, z, lax.rem(y + d, NY), c)),
            send(b, b, two_s.at[1, d], two_r.at[1, d], device(lax.rem(x + d, NX), z, y, c)),
        )

    seconds = [two(d) for d in (1, 3, 2)]
    for pair in seconds:
        for copy in pair:
            copy.start()

    column, row, last = [], [], []
    for s in range(2):
        a, b, l = segments(F[s])
        column.append(a)
        row.append(b)
        last.append(l)
    for s in range(2):
        keep = jnp.where(last[s] > 0, 0.0, 1.0)
        KB[s] = jnp.broadcast_to(keep, (8, HEAD))
    for pair in seconds:
        for copy in pair:
            copy.wait()

    def three_a(d):
        a = W.at[0, x]
        return send(a, a, three_s.at[0, d], three_r.at[0, d], device(lax.rem(x + d, NX), z, y, c))

    def three_b(d, part):
        b = W.at[1, part, :, y]
        return send(b, b, three_s.at[1 + part, d], three_r.at[1 + part, d], device(x, z, lax.rem(y + d, NY), c))

    for d in (1, 3, 2):
        three_a(d).start()
    for part in range(NX):
        for d in (1, 3, 2):
            three_b(d, part).start()

    swap_t.wait()
    depth = NZ * NY * 16

    def project(h, part):
        cols = pl.ds(pl.multiple_of(part * depth, depth), depth)
        rows = jnp.concatenate([T[0, :, cols], T[1, :, cols]], axis=0)
        return jnp.dot(rows, W[h, part].reshape(depth, 2 * HEAD), preferred_element_type=F32)

    acc[0] = project(0, x)
    for d in (1, 3, 2):
        three_a(d).wait()
        acc[0] += project(0, lax.rem(x - d + NX, NX))
    acc[1] = jnp.zeros_like(acc[1])
    for part in range(NX):
        for d in (1, 3, 2):
            three_b(d, part).wait()
        acc[1] += project(1, part)

    place = lax.rem(z + NZ // 2, GROUP)
    base = lax.rem(x + NX - jnp.where(place < GROUP // 2, 0, 1), NX)

    def member(p, core):
        return device(
            lax.rem(base + p // (GROUP // 2), NX), lax.rem(p + NZ // 2, NZ), y, core
        )

    def keep_copy(d):
        return send(KB, KR.at[place], k_s.at[d], k_r.at[d], member(lax.rem(place + d, GROUP), c))

    def one_copy(d):
        p = lax.rem(place + d, GROUP)
        return send(ST.at[p], SR.at[place], s1_s.at[d], s1_r.at[d], member(p, c))

    def keep_start(d, carry):
        keep_copy(d).start()
        return carry

    def one_start(d, carry):
        one_copy(d).start()
        return carry

    def one_wait(d, carry):
        one_copy(d).wait()
        keep_copy(d).wait()
        return carry

    lax.fori_loop(1, GROUP, keep_start, 0)
    KR[place] = KB[...]

    for s in range(2):
        tail = (column[s] == last[s]).astype(F32)
        for h in range(2):
            part = acc[h, s * HEAD : (s + 1) * HEAD, :]
            key = phi(part[:, :HEAD]).astype(BF16)
            value = part[:, HEAD:].astype(BF16)
            KV[s, 2 * c + h, 0] = key
            KV[s, 2 * c + h, 1] = value
            masked = (key.astype(F32) * tail).astype(BF16)
            state = lax.dot_general(masked, value, (((0,), (0,)), ((), ())), preferred_element_type=F32)
            slot = (s * 2 + h) * 4
            ST[slot : slot + 4] = state.astype(BF16).reshape(4, HEAD // 4, HEAD)
    lax.fori_loop(1, GROUP, one_start, 0)
    SR[place] = ST[place]
    given = KV.at[other, pl.ds(2 * c, 2)]
    swap_kv = send(given, given, pair_s.at[3], pair_r.at[3], sibling)
    swap_kv.start()

    loads[4].wait()
    my_column = jnp.where(c == 0, column[0], column[1])
    my_row = jnp.where(c == 0, row[0], row[1])
    t = lax.broadcasted_iota(jnp.int32, (HEAD, HEAD), 0)
    u = lax.broadcasted_iota(jnp.int32, (HEAD, HEAD), 1)
    allowed = (u <= t) & (my_column == my_row)
    Q[...] = phi(Q[...].astype(F32)).astype(BF16)
    swap_kv.wait()
    for h in range(4):
        query = Q[:, h * HEAD : (h + 1) * HEAD]
        key, value = KV[c, h, 0], KV[c, h, 1]
        scores = lax.dot_general(query, key, (((1,), (1,)), ((), ())), preferred_element_type=F32)
        scores = jnp.where(allowed, scores, 0.0).astype(BF16)
        MIX[h] = jnp.dot(scores, value, preferred_element_type=F32)

    lax.fori_loop(1, GROUP, one_wait, 0)
    seq = place // (GROUP // 2)

    def prefix(b, carried):
        CS[b] = carried.astype(BF16)
        return KR[b, seq][0:1, :] * carried + SR[b].astype(F32)

    lax.fori_loop(0, GROUP, prefix, jnp.zeros((HEAD // 4, HEAD), F32))

    mine_at = lax.rem(place, GROUP // 2)
    target = CR.at[2 * c + mine_at // 4, lax.rem(mine_at, 4)]
    index = c * 8 + mine_at

    def back_copy(d):
        p = lax.rem(place + d, GROUP)
        return send(CS.at[p], target, s2_s.at[d], s2_r.at[index], member(p, seq))

    def back_start(d, carry):
        back_copy(d).start()
        return carry

    def back_wait(d, carry):
        back_copy(d).wait_send()
        return carry

    own = pltpu.make_async_copy(CS.at[place], target, s2_r.at[index])

    @pl.when(seq == c)
    def _():
        own.start()

    @pl.when(seq != c)
    def _():
        back_copy(0).start()

    lax.fori_loop(1, GROUP, back_start, 0)

    def arrive(i, carry):
        send(CS.at[0], CR.at[i // 4, lax.rem(i, 4)], s2_s.at[0], s2_r.at[i], sibling).wait_recv()
        return carry

    lax.fori_loop(0, GROUP, arrive, 0)
    first = (my_column == 0).astype(F32)
    for h in range(4):
        query = Q[:, h * HEAD : (h + 1) * HEAD]
        state = CR[h].reshape(HEAD, HEAD)
        mixed = MIX[h] + first * jnp.dot(query, state, preferred_element_type=F32)
        scale = lax.rsqrt(jnp.mean(mixed * mixed, axis=-1, keepdims=True) + 1e-06)
        cut = slice(h * HEAD, (h + 1) * HEAD)
        out[:, cut] = (mixed * scale * gain[:, cut]).astype(BF16)

    @pl.when(seq != c)
    def _():
        back_copy(0).wait_send()

    lax.fori_loop(1, GROUP, back_wait, 0)


def on_device(tokens, queries, flags, w_key, w_value, norm_gain):
    count, width = queries.shape[1:]
    dma = pltpu.SemaphoreType.DMA
    any_spec = pl.BlockSpec(memory_space=pl.ANY)
    vmem_spec = pl.BlockSpec(memory_space=pltpu.VMEM)
    attended = pl.pallas_call(
        kernel,
        out_shape=jax.ShapeDtypeStruct((count, width), BF16),
        in_specs=[any_spec, any_spec, any_spec, any_spec, any_spec, vmem_spec],
        out_specs=vmem_spec,
        scratch_shapes=[
            pltpu.VMEM((2, count, tokens.shape[2]), BF16),
            pltpu.VMEM((count, width), BF16),
            pltpu.VMEM((2, 1, count), jnp.int32),
            pltpu.VMEM((2, 2, 8, width), BF16),
            pltpu.VMEM((2, NX, NZ, NY, 16, 2 * HEAD), BF16),
            pltpu.VMEM((2, 2 * count, 2 * HEAD), F32),
            pltpu.VMEM((2, 4, 2, count, HEAD), BF16),
            pltpu.VMEM((2, 8, HEAD), F32),
            pltpu.VMEM((GROUP, 2, 8, HEAD), F32),
            pltpu.VMEM((GROUP, HEAD // 4, HEAD), BF16),
            pltpu.VMEM((GROUP, HEAD // 4, HEAD), BF16),
            pltpu.VMEM((GROUP, HEAD // 4, HEAD), BF16),
            pltpu.VMEM((4, 4, HEAD // 4, HEAD), BF16),
            pltpu.VMEM((4, count, HEAD), F32),
            dma((5,)),
            dma((4,)),
            dma((4,)),
            dma((NZ,)),
            dma((NZ,)),
            dma((2, 4)),
            dma((2, 4)),
            dma((5, 4)),
            dma((5, 4)),
            dma((GROUP,)),
            dma((GROUP,)),
            dma((GROUP,)),
            dma((GROUP,)),
            dma((GROUP,)),
            dma((GROUP,)),
        ],
        compiler_params=pltpu.CompilerParams(
            collective_id=0, has_side_effects=True, vmem_limit_bytes=40 << 20
        ),
        name="attention",
    )(tokens[0], queries[0], flags, w_key, w_value, norm_gain.reshape(1, width))
    return attended.reshape(1, count, width)


def solution(mesh):
    in_specs = (
        P("fsdp", "ctx", None),
        P("fsdp", "ctx", None),
        P("fsdp", "ctx"),
        P(("ctx", "fsdp"), None),
        P(("ctx", "fsdp"), None),
        P(),
    )
    out_specs = P("fsdp", "ctx", None)
    return jax.shard_map(
        on_device, mesh=mesh, in_specs=in_specs, out_specs=out_specs, check_vma=False
    )
```

```python
import functools

import jax
import jax.numpy as jnp
from jax import lax
from jax.experimental import pallas as pl
from jax.experimental.pallas import tpu as pltpu
from jax.sharding import PartitionSpec as P

HEAD = 128
MESH = pl.DeviceIdType.MESH
NX, NY, NZ = 4, 4, 16
GROUP = 16
F32, BF16 = jnp.float32, jnp.bfloat16


def device(x, z, y, c):
    return (x * NZ + z, y * 2 + c)


def phi(u):
    return jnp.where(u > 0, u + 1.0, jnp.exp(jnp.minimum(u, 0.0)))


def segments(marks):
    n = marks.shape[1]
    t = lax.broadcasted_iota(jnp.int32, (n, n), 0)
    s = lax.broadcasted_iota(jnp.int32, (n, n), 1)
    wide = jnp.broadcast_to(marks, (n, n)).astype(F32)
    column = jnp.sum(jnp.where(s <= t, wide, 0.0), axis=1, keepdims=True)
    upright = jnp.sum(jnp.where(s == t, wide, 0.0), axis=1, keepdims=True)
    row = jnp.sum(jnp.where(t <= s, jnp.broadcast_to(upright, (n, n)), 0.0), axis=0, keepdims=True)
    last = jnp.sum(marks.astype(F32), axis=1, keepdims=True)
    return column, row, last


def kernel(
    tok, qry, flg, wk, wv, gain, out,
    T, Q, F, G, WB, W, acc, KV, KG, ST, SR, CS, CR, MIX,
    loc, pair_s, pair_r, z_s, z_r, k_s, k_r, two_s, two_r, three_s, three_r, s1_s, s1_r, s2_s, s2_r,
):
    ctx, fsdp = lax.axis_index("ctx"), lax.axis_index("fsdp")
    x, z = ctx // NZ, lax.rem(ctx, NZ)
    y, c = fsdp // 2, lax.rem(fsdp, 2)
    quad, low = z // 4, lax.rem(z, 4)
    other = 1 - c
    sibling = device(x, z, y, other)

    def at_x(d):
        return device(lax.rem(x + d, NX), z, y, c)

    def at_y(d):
        return device(x, z, lax.rem(y + d, NY), c)

    def at_z(d):
        return device(x, lax.rem(z + d, NZ), y, c)

    def in_quad(d):
        return device(x, quad * 4 + lax.rem(low + d, 4), y, c)

    loads = [
        pltpu.make_async_copy(wk, WB.at[c, 0], loc.at[0]),
        pltpu.make_async_copy(wv, WB.at[c, 1], loc.at[1]),
        pltpu.make_async_copy(flg, F.at[c], loc.at[2]),
        pltpu.make_async_copy(tok, T.at[c], loc.at[3]),
        pltpu.make_async_copy(qry, Q, loc.at[4]),
        pltpu.make_async_copy(gain, G, loc.at[5]),
    ]
    for load in loads:
        load.start()

    barrier = pltpu.get_barrier_semaphore()
    greeted = [sibling, at_z(4), at_z(12)]
    for d in range(1, 4):
        greeted += [at_x(d), at_y(d), in_quad(d)]
    for to in greeted:
        pl.semaphore_signal(barrier, inc=1, device_id=to, device_id_type=MESH)
    for load in loads[:3]:
        load.wait()
    pl.semaphore_wait(barrier, len(greeted))

    started = []

    def send(src, dst, ss, rs, to):
        return pltpu.make_async_remote_copy(
            src_ref=src, dst_ref=dst, send_sem=ss, recv_sem=rs, device_id=to, device_id_type=MESH
        )

    def same(ref, ss, rs, to):
        return send(ref, ref, ss, rs, to)

    def start(copies):
        for copy in copies:
            copy.start()
            started.append(copy)

    def arrive(copies):
        for copy in copies:
            copy.wait_recv()

    swap_w = same(WB.at[c], pair_s.at[0], pair_r.at[0], sibling)
    swap_f = same(F.at[c], pair_s.at[1], pair_r.at[1], sibling)
    swap_t = same(T.at[c], pair_s.at[2], pair_r.at[2], sibling)
    start([swap_w, swap_f])
    arrive([swap_w])
    both = jnp.concatenate([WB[0].astype(F32), WB[1].astype(F32)], axis=1)
    mine = jnp.where(c == 0, both[:, :, : 2 * HEAD], both[:, :, 2 * HEAD :]).astype(BF16)
    for h in range(2):
        cut = slice(h * HEAD, (h + 1) * HEAD)
        W[h, x, z, y] = jnp.concatenate([mine[0, :, cut], mine[1, :, cut]], axis=1)

    def four(r):
        return pl.ds(lax.rem(quad + r, 4) * 4, 4)

    def half(r, side):
        return pl.ds(lax.rem(quad + r, 4) * 4 + 2 * side, 2)

    z0 = [same(W.at[:, x, z, y], z_s.at[d], z_r.at[d], in_quad(d)) for d in range(1, 4)]
    z_up = same(W.at[:, x, four(0), y], z_s.at[4], z_r.at[4], at_z(4))
    z_down = same(W.at[:, x, four(0), y], z_s.at[5], z_r.at[5], at_z(12))
    z_far = [
        same(W.at[:, x, half(1, 0), y], z_s.at[6], z_r.at[6], at_z(12)),
        same(W.at[:, x, half(3, 1), y], z_s.at[7], z_r.at[7], at_z(4)),
    ]
    k0 = [same(KG.at[x, z], k_s.at[d], k_r.at[d], in_quad(d)) for d in range(1, 4)]
    k_up = same(KG.at[x, four(0)], k_s.at[4], k_r.at[4], at_z(4))
    k_down = same(KG.at[x, four(0)], k_s.at[5], k_r.at[5], at_z(12))
    k_far = same(KG.at[x, four(1)], k_s.at[6], k_r.at[6], at_z(12))
    k_x = [same(KG.at[x], k_s.at[7 + i], k_r.at[7 + i], at_x(d)) for i, d in enumerate((1, 3))]

    def two(r):
        a, b = W.at[0, x, four(r), y], W.at[1, x, four(r), y]
        return [same(a, two_s.at[r, 0, d], two_r.at[r, 0, d], at_y(d)) for d in (1, 3, 2)] + [
            same(b, two_s.at[r, 1, d], two_r.at[r, 1, d], at_x(d)) for d in (1, 3, 2)
        ]

    def three(r):
        a, b = W.at[0, x, four(r)], W.at[1, :, four(r), y]
        return [same(a, three_s.at[r, 0, d], three_r.at[r, 0, d], at_x(d)) for d in (1, 3)] + [
            same(b, three_s.at[r, 1, d], three_r.at[r, 1, d], at_y(d)) for d in (1, 3)
        ]

    def far(r):
        to = 1 if r in (0, 3) else 3
        a = W.at[0, lax.rem(x + 4 - to, NX), four(r)]
        b = W.at[1, :, four(r), lax.rem(y + 4 - to, NY)]
        return [
            same(a, three_s.at[r, 0, 2], three_r.at[r, 0, 2], at_x(to)),
            same(b, three_s.at[r, 1, 2], three_r.at[r, 1, 2], at_y(to)),
        ]

    depth = 4 * NY * 16

    def project(h, part, r):
        q = lax.rem(quad + r, 4)
        cols = pl.ds(pl.multiple_of((part * 4 + q) * depth, depth), depth)
        rows = T[:, :, cols].reshape(2 * HEAD, depth)
        acc[h] += jnp.dot(
            rows, W[h, part, four(r)].reshape(depth, 2 * HEAD), preferred_element_type=F32
        )

    def near_a(r):
        def one(i, carry):
            project(0, lax.rem(x + 3 + i, NX), r)
            return carry

        lax.fori_loop(0, 3, one, 0)

    def rest(r):
        project(0, lax.rem(x + 2, NX), r)

        def one(i, carry):
            project(1, i, r)
            return carry

        lax.fori_loop(0, NX, one, 0)

    start(z0)
    loads[3].wait()
    start([swap_t])
    arrive([swap_f])
    column, row, last = [], [], []
    for s in range(2):
        a, b, l = segments(F[s])
        column.append(a)
        row.append(b)
        last.append(l)
    keeps = [jnp.broadcast_to(jnp.where(l > 0, 0.0, 1.0), (4, HEAD)) for l in last]
    KG[x, z] = jnp.concatenate(keeps, axis=0)
    arrive(z0)
    start([z_up, z_down])
    start(two(0))
    start(k0)
    acc[...] = jnp.zeros_like(acc)
    arrive(k0)
    start([k_up, k_down])
    arrive(two(0))
    start(three(0))
    arrive([z_up])
    start([z_far[1]])
    start(two(3))
    arrive([z_down])
    start([z_far[0]])
    start(two(1))
    arrive([k_up, k_down])
    start([k_far])
    arrive(two(3))
    start(three(3))
    arrive(three(0))
    start(far(0))
    arrive(two(1))
    start(three(1))
    arrive(z_far)
    start(two(2))
    arrive([k_far])
    start(k_x)
    arrive([swap_t])
    near_a(0)
    arrive(three(3))
    start(far(3))
    near_a(3)
    arrive(two(2))
    start(three(2))
    arrive(three(1))
    start(far(1))
    arrive(far(0))
    rest(0)
    near_a(1)
    arrive(far(3))
    rest(3)
    arrive(three(2))
    start(far(2))
    near_a(2)
    arrive(far(1))
    rest(1)
    arrive(k_x)
    arrive(far(2))
    rest(2)

    place = lax.rem(z + NZ // 2, GROUP)
    base = lax.rem(x + NX - jnp.where(place < GROUP // 2, 0, 1), NX)

    def member_x(p):
        return lax.rem(base + p // (GROUP // 2), NX)

    def member_z(p):
        return lax.rem(p + NZ // 2, NZ)

    def member(p, core):
        return device(member_x(p), member_z(p), y, core)

    def one_copy(d):
        p = lax.rem(place + d, GROUP)
        return send(ST.at[p], SR.at[place], s1_s.at[d], s1_r.at[d], member(p, c))

    def one_start(d, carry):
        one_copy(d).start()
        return carry

    def one_wait(d, carry):
        one_copy(d).wait()
        return carry

    for s in range(2):
        tail = (column[s] == last[s]).astype(F32)
        for h in range(2):
            part = acc[h, s * HEAD : (s + 1) * HEAD, :]
            key = phi(part[:, :HEAD]).astype(BF16)
            value = part[:, HEAD:].astype(BF16)
            KV[s, 2 * c + h, 0] = key
            KV[s, 2 * c + h, 1] = value
            masked = (key.astype(F32) * tail).astype(BF16)
            state = lax.dot_general(masked, value, (((0,), (0,)), ((), ())), preferred_element_type=F32)
            slot = (s * 2 + h) * 4
            ST[slot : slot + 4] = state.astype(BF16).reshape(4, HEAD // 4, HEAD)
    lax.fori_loop(1, GROUP, one_start, 0)
    SR[place] = ST[place]
    swap_kv = same(KV.at[other, pl.ds(2 * c, 2)], pair_s.at[3], pair_r.at[3], sibling)
    start([swap_kv])

    loads[4].wait()
    loads[5].wait()
    my_column = jnp.where(c == 0, column[0], column[1])
    my_row = jnp.where(c == 0, row[0], row[1])
    t = lax.broadcasted_iota(jnp.int32, (HEAD, HEAD), 0)
    u = lax.broadcasted_iota(jnp.int32, (HEAD, HEAD), 1)
    allowed = (u <= t) & (my_column == my_row)
    Q[...] = phi(Q[...].astype(F32)).astype(BF16)
    arrive([swap_kv])
    for h in range(4):
        query = Q[:, h * HEAD : (h + 1) * HEAD]
        key, value = KV[c, h, 0], KV[c, h, 1]
        scores = lax.dot_general(query, key, (((1,), (1,)), ((), ())), preferred_element_type=F32)
        scores = jnp.where(allowed, scores, 0.0).astype(BF16)
        MIX[h] = jnp.dot(scores, value, preferred_element_type=F32)

    lax.fori_loop(1, GROUP, one_wait, 0)
    seq = place // (GROUP // 2)

    def prefix(b, carried):
        CS[b] = carried.astype(BF16)
        tile = KG[member_x(b), member_z(b)]
        keep = jnp.where(seq == 0, tile[0:1], tile[4:5])
        return keep * carried + SR[b].astype(F32)

    lax.fori_loop(0, GROUP, prefix, jnp.zeros((HEAD // 4, HEAD), F32))

    mine_at = lax.rem(place, GROUP // 2)
    target = CR.at[2 * c + mine_at // 4, lax.rem(mine_at, 4)]
    index = c * 8 + mine_at

    def back_copy(d):
        p = lax.rem(place + d, GROUP)
        return send(CS.at[p], target, s2_s.at[d], s2_r.at[index], member(p, seq))

    def back_start(d, carry):
        back_copy(d).start()
        return carry

    def back_wait(d, carry):
        back_copy(d).wait_send()
        return carry

    own = pltpu.make_async_copy(CS.at[place], target, s2_r.at[index])

    @pl.when(seq == c)
    def _():
        own.start()

    @pl.when(seq != c)
    def _():
        back_copy(0).start()

    lax.fori_loop(1, GROUP, back_start, 0)

    def back_arrive(i, carry):
        send(CS.at[0], CR.at[i // 4, lax.rem(i, 4)], s2_s.at[0], s2_r.at[i], sibling).wait_recv()
        return carry

    for copy in started:
        copy.wait_send()
    lax.fori_loop(0, GROUP, back_arrive, 0)
    first = (my_column == 0).astype(F32)
    for h in range(4):
        query = Q[:, h * HEAD : (h + 1) * HEAD]
        state = CR[h].reshape(HEAD, HEAD)
        mixed = MIX[h] + first * jnp.dot(query, state, preferred_element_type=F32)
        scale = lax.rsqrt(jnp.mean(mixed * mixed, axis=-1, keepdims=True) + 1e-06)
        cut = slice(h * HEAD, (h + 1) * HEAD)
        out[:, cut] = (mixed * scale * G[:, cut]).astype(BF16)

    @pl.when(seq != c)
    def _():
        back_copy(0).wait_send()

    lax.fori_loop(1, GROUP, back_wait, 0)


def on_device(tokens, queries, flags, w_key, w_value, norm_gain):
    count, width = queries.shape[1:]
    dma = pltpu.SemaphoreType.DMA
    any_spec = pl.BlockSpec(memory_space=pltpu.HBM)
    vmem_spec = pl.BlockSpec(memory_space=pltpu.VMEM)
    attended = pl.pallas_call(
        kernel,
        out_shape=jax.ShapeDtypeStruct((count, width), BF16),
        in_specs=[any_spec] * 6,
        out_specs=vmem_spec,
        scratch_shapes=[
            pltpu.VMEM((2, count, tokens.shape[2]), BF16),
            pltpu.VMEM((count, width), BF16),
            pltpu.VMEM((2, 1, count), jnp.int32),
            pltpu.VMEM((1, width), F32),
            pltpu.VMEM((2, 2, 8, width), BF16),
            pltpu.VMEM((2, NX, NZ, NY, 16, 2 * HEAD), BF16),
            pltpu.VMEM((2, 2 * count, 2 * HEAD), F32),
            pltpu.VMEM((2, 4, 2, count, HEAD), BF16),
            pltpu.VMEM((NX, NZ, 8, HEAD), F32),
            pltpu.VMEM((GROUP, HEAD // 4, HEAD), BF16),
            pltpu.VMEM((GROUP, HEAD // 4, HEAD), BF16),
            pltpu.VMEM((GROUP, HEAD // 4, HEAD), BF16),
            pltpu.VMEM((4, 4, HEAD // 4, HEAD), BF16),
            pltpu.VMEM((4, count, HEAD), F32),
            dma((6,)),
            dma((4,)),
            dma((4,)),
            dma((8,)),
            dma((8,)),
            dma((9,)),
            dma((9,)),
            dma((4, 2, 4)),
            dma((4, 2, 4)),
            dma((4, 2, 4)),
            dma((4, 2, 4)),
            dma((GROUP,)),
            dma((GROUP,)),
            dma((GROUP,)),
            dma((GROUP,)),
        ],
        compiler_params=pltpu.CompilerParams(
            collective_id=0, has_side_effects=True, vmem_limit_bytes=62 << 20
        ),
        name="attention",
    )(tokens[0], queries[0], flags, w_key, w_value, norm_gain.reshape(1, width))
    return attended.reshape(1, count, width)


def solution(mesh):
    in_specs = (
        P("fsdp", "ctx", None),
        P("fsdp", "ctx", None),
        P("fsdp", "ctx"),
        P(("ctx", "fsdp"), None),
        P(("ctx", "fsdp"), None),
        P(),
    )
    out_specs = P("fsdp", "ctx", None)
    return jax.shard_map(
        on_device, mesh=mesh, in_specs=in_specs, out_specs=out_specs, check_vma=False
    )
```

```python
import functools

import jax
import jax.numpy as jnp
from jax import lax
from jax.experimental import pallas as pl
from jax.experimental.pallas import tpu as pltpu
from jax.sharding import PartitionSpec as P

HEAD = 128
MESH = pl.DeviceIdType.MESH
NX, NY, NZ = 4, 4, 16
GROUP = 16
F32, BF16 = jnp.float32, jnp.bfloat16


def device(x, z, y, c):
    return (x * NZ + z, y * 2 + c)


def phi(u):
    return jnp.where(u > 0, u + 1.0, jnp.exp(jnp.minimum(u, 0.0)))


def segments(marks):
    n = marks.shape[1]
    t = lax.broadcasted_iota(jnp.int32, (n, n), 0)
    s = lax.broadcasted_iota(jnp.int32, (n, n), 1)
    wide = jnp.broadcast_to(marks, (n, n)).astype(F32)
    column = jnp.sum(jnp.where(s <= t, wide, 0.0), axis=1, keepdims=True)
    upright = jnp.sum(jnp.where(s == t, wide, 0.0), axis=1, keepdims=True)
    row = jnp.sum(jnp.where(t <= s, jnp.broadcast_to(upright, (n, n)), 0.0), axis=0, keepdims=True)
    last = jnp.sum(marks.astype(F32), axis=1, keepdims=True)
    return column, row, last


def kernel(
    tok, qry, flg, wk, wv, gain, out,
    T, Q, F, G, WB, W, acc, KV, TL, KB, KR, ST, SR, CS, CR, MIX,
    loc, pair_s, pair_r, hop_s, hop_r, z_s, z_r, k_s, k_r, two_s, two_r, three_s, three_r, s1_s, s1_r, s2_s, s2_r,
):
    ctx, fsdp = lax.axis_index("ctx"), lax.axis_index("fsdp")
    x, z = ctx // NZ, lax.rem(ctx, NZ)
    y, c = fsdp // 2, lax.rem(fsdp, 2)
    quad, low = z // 4, lax.rem(z, 4)
    other = 1 - c
    sibling = device(x, z, y, other)

    def at_x(d):
        return device(lax.rem(x + d, NX), z, y, c)

    def at_y(d):
        return device(x, z, lax.rem(y + d, NY), c)

    def at_z(d):
        return device(x, lax.rem(z + d, NZ), y, c)

    def in_quad(d):
        return device(x, quad * 4 + lax.rem(low + d, 4), y, c)

    loads = [
        pltpu.make_async_copy(wk, WB.at[c, 0], loc.at[0]),
        pltpu.make_async_copy(wv, WB.at[c, 1], loc.at[1]),
        pltpu.make_async_copy(flg, F.at[c], loc.at[2]),
        pltpu.make_async_copy(tok, T.at[c], loc.at[3]),
        pltpu.make_async_copy(qry, Q, loc.at[4]),
        pltpu.make_async_copy(gain, G, loc.at[5]),
    ]
    for load in loads:
        load.start()

    barrier = pltpu.get_barrier_semaphore()

    def greet(to):
        pl.semaphore_signal(barrier, inc=1, device_id=to, device_id_type=MESH)

    def greet_xy(d, carry):
        greet(at_x(d))
        greet(at_y(d))
        greet(in_quad(d))
        return carry

    lax.fori_loop(1, 4, greet_xy, 0)
    greet(sibling)
    greet(at_z(4))
    greet(at_z(12))
    for load in loads[:3]:
        load.wait()
    pl.semaphore_wait(barrier, 12)

    def send(src, dst, ss, rs, to):
        return pltpu.make_async_remote_copy(
            src_ref=src, dst_ref=dst, send_sem=ss, recv_sem=rs, device_id=to, device_id_type=MESH
        )

    def same(ref, ss, rs, to):
        return send(ref, ref, ss, rs, to)

    def start(copies):
        for copy in copies:
            copy.start()

    def arrive(copies):
        for copy in copies:
            copy.wait_recv()

    swap_w = same(WB.at[c], pair_s.at[0], pair_r.at[0], sibling)
    swap_f = same(F.at[c], pair_s.at[1], pair_r.at[1], sibling)
    swap_t = same(T.at[c], pair_s.at[2], pair_r.at[2], sibling)
    start([swap_w, swap_f])
    arrive([swap_w])
    both = jnp.concatenate([WB[0].astype(F32), WB[1].astype(F32)], axis=1)
    mine = jnp.where(c == 0, both[:, :, : 2 * HEAD], both[:, :, 2 * HEAD :]).astype(BF16)
    for h in range(2):
        cut = slice(h * HEAD, (h + 1) * HEAD)
        W[h, x, z, y] = jnp.concatenate([mine[0, :, cut], mine[1, :, cut]], axis=1)

    def four(r):
        return pl.ds(lax.rem(quad + r, 4) * 4, 4)

    def hop(d, ahead, k):
        piece = W.at[:, x, lax.rem(z + ahead, NZ), y]
        return same(piece, hop_s.at[k], hop_r.at[k], at_z(d))

    hops = [hop(4, 0, 0), hop(12, 0, 1), hop(12, 4, 2)]

    def share(r):
        piece = W.at[:, x, lax.rem(z + 4 * r, NZ), y]
        return [same(piece, z_s.at[r, d], z_r.at[r, d], in_quad(d)) for d in range(1, 4)]

    def two(r):
        a, b = W.at[0, x, four(r), y], W.at[1, x, four(r), y]
        return [same(a, two_s.at[r, 0, d], two_r.at[r, 0, d], at_y(d)) for d in (1, 3, 2)] + [
            same(b, two_s.at[r, 1, d], two_r.at[r, 1, d], at_x(d)) for d in (1, 3, 2)
        ]

    def three(r):
        a, b = W.at[0, x, four(r)], W.at[1, :, four(r), y]
        return [same(a, three_s.at[r, 0, d], three_r.at[r, 0, d], at_x(d)) for d in (1, 3)] + [
            same(b, three_s.at[r, 1, d], three_r.at[r, 1, d], at_y(d)) for d in (1, 3)
        ]

    def far(r):
        to = jnp.where(lax.rem(r, 2) == 0, 1, 3)
        a = W.at[0, lax.rem(x + 4 - to, NX), four(r)]
        b = W.at[1, :, four(r), lax.rem(y + 4 - to, NY)]
        return [
            same(a, three_s.at[r, 0, 2], three_r.at[r, 0, 2], at_x(to)),
            same(b, three_s.at[r, 1, 2], three_r.at[r, 1, 2], at_y(to)),
        ]

    depth = 4 * NY * 16

    def project(h, part, r):
        q = lax.rem(quad + r, 4)
        cols = pl.ds(pl.multiple_of((part * 4 + q) * depth, depth), depth)
        rows = T[:, :, cols].reshape(2 * HEAD, depth)
        acc[h] += jnp.dot(
            rows, W[h, part, four(r)].reshape(depth, 2 * HEAD), preferred_element_type=F32
        )

    def near_a(r):
        def one(i, carry):
            project(0, lax.rem(x + 3 + i, NX), r)
            return carry

        lax.fori_loop(0, 3, one, 0)

    def rest(r):
        project(0, lax.rem(x + 2, NX), r)

        def one(i, carry):
            project(1, i, r)
            return carry

        lax.fori_loop(0, NX, one, 0)

    place = lax.rem(z + NZ // 2, GROUP)
    base = lax.rem(x + NX - jnp.where(place < GROUP // 2, 0, 1), NX)

    def member(p, core):
        return device(lax.rem(base + p // (GROUP // 2), NX), lax.rem(p + NZ // 2, NZ), y, core)

    def keep_copy(d):
        return send(KB, KR.at[place], k_s.at[d], k_r.at[d], member(lax.rem(place + d, GROUP), c))

    def keep_start(d, carry):
        keep_copy(d).start()
        return carry

    start(hops[:2])
    start(share(0))
    loads[3].wait()
    start([swap_t])
    arrive([swap_f])
    column, row, last = [], [], []
    for s in range(2):
        a, b, l = segments(F[s])
        column.append(a)
        row.append(b)
        last.append(l)
    keeps = [jnp.broadcast_to(jnp.where(l > 0, 0.0, 1.0), (4, HEAD)) for l in last]
    KB[...] = jnp.concatenate(keeps, axis=0)
    KR[place] = KB[...]
    acc[...] = jnp.zeros_like(acc)

    arrive(share(0))
    start(two(0))
    arrive(hops[:2])
    start(hops[2:])
    start(share(1))
    start(share(3))
    arrive(two(0))
    start(three(0))
    arrive(hops[2:])
    start(share(2))
    arrive(share(1))
    start(two(1))
    arrive(share(3))
    start(two(3))
    arrive(three(0))
    start(far(0))
    arrive(share(2))
    start(two(2))
    arrive(two(1))
    start(three(1))
    arrive(two(3))
    start(three(3))
    arrive([swap_t])
    near_a(0)
    arrive(far(0))
    rest(0)
    arrive(two(2))
    start(three(2))
    arrive(three(1))
    start(far(1))
    arrive(three(3))
    start(far(3))
    near_a(1)
    near_a(3)
    arrive(three(2))
    start(far(2))
    lax.fori_loop(1, GROUP, keep_start, 0)
    arrive(far(1))
    rest(1)
    arrive(far(3))
    rest(3)
    near_a(2)
    arrive(far(2))
    rest(2)

    def one_copy(d):
        p = lax.rem(place + d, GROUP)
        return send(ST.at[p], SR.at[place], s1_s.at[d], s1_r.at[d], member(p, c))

    def one_start(d, carry):
        one_copy(d).start()
        return carry

    def one_wait(d, carry):
        one_copy(d).wait()
        keep_copy(d).wait()
        return carry

    for s in range(2):
        TL[s] = jnp.broadcast_to((column[s] == last[s]).astype(F32), (HEAD, HEAD))

    def states(i, carry):
        s, h = i // 2, lax.rem(i, 2)
        part = acc[h, pl.ds(pl.multiple_of(s * HEAD, HEAD), HEAD), :]
        key = phi(part[:, :HEAD]).astype(BF16)
        value = part[:, HEAD:].astype(BF16)
        KV[s, 2 * c + h, 0] = key
        KV[s, 2 * c + h, 1] = value
        masked = (key.astype(F32) * TL[s]).astype(BF16)
        state = lax.dot_general(masked, value, (((0,), (0,)), ((), ())), preferred_element_type=F32)
        ST[pl.ds(4 * i, 4)] = state.astype(BF16).reshape(4, HEAD // 4, HEAD)
        return carry

    lax.fori_loop(0, 4, states, 0)
    lax.fori_loop(1, GROUP, one_start, 0)
    SR[place] = ST[place]
    swap_kv = same(KV.at[other, pl.ds(2 * c, 2)], pair_s.at[3], pair_r.at[3], sibling)
    start([swap_kv])

    loads[4].wait()
    loads[5].wait()
    my_column = jnp.where(c == 0, column[0], column[1])
    my_row = jnp.where(c == 0, row[0], row[1])
    t = lax.broadcasted_iota(jnp.int32, (HEAD, HEAD), 0)
    u = lax.broadcasted_iota(jnp.int32, (HEAD, HEAD), 1)
    allowed = (u <= t) & (my_column == my_row)
    Q[...] = phi(Q[...].astype(F32)).astype(BF16)
    arrive([swap_kv])
    mask = allowed.astype(F32)

    def inside(h, carry):
        query = Q[:, pl.ds(pl.multiple_of(h * HEAD, HEAD), HEAD)]
        key, value = KV[c, h, 0], KV[c, h, 1]
        scores = lax.dot_general(query, key, (((1,), (1,)), ((), ())), preferred_element_type=F32)
        scores = (scores * mask).astype(BF16)
        MIX[h] = jnp.dot(scores, value, preferred_element_type=F32)
        return carry

    lax.fori_loop(0, 4, inside, 0)
    lax.fori_loop(1, GROUP, one_wait, 0)
    seq = place // (GROUP // 2)

    def prefix(b, carried):
        CS[b] = carried.astype(BF16)
        tile = KR[b]
        keep = jnp.where(seq == 0, tile[0:1], tile[4:5])
        return keep * carried + SR[b].astype(F32)

    lax.fori_loop(0, GROUP, prefix, jnp.zeros((HEAD // 4, HEAD), F32))

    mine_at = lax.rem(place, GROUP // 2)
    target = CR.at[2 * c + mine_at // 4, lax.rem(mine_at, 4)]
    index = c * 8 + mine_at

    def back_copy(d):
        p = lax.rem(place + d, GROUP)
        return send(CS.at[p], target, s2_s.at[d], s2_r.at[index], member(p, seq))

    def back_start(d, carry):
        back_copy(d).start()
        return carry

    def back_wait(d, carry):
        back_copy(d).wait_send()
        return carry

    own = pltpu.make_async_copy(CS.at[place], target, s2_r.at[index])

    @pl.when(seq == c)
    def _():
        own.start()

    @pl.when(seq != c)
    def _():
        back_copy(0).start()

    lax.fori_loop(1, GROUP, back_start, 0)

    def back_arrive(i, carry):
        send(CS.at[0], CR.at[i // 4, lax.rem(i, 4)], s2_s.at[0], s2_r.at[i], sibling).wait_recv()
        return carry

    def drain(r, carry):
        for copy in share(r) + two(r) + three(r) + far(r):
            copy.wait_send()
        return carry

    lax.fori_loop(0, 4, drain, 0)
    for copy in hops + [swap_w, swap_f, swap_t, swap_kv]:
        copy.wait_send()
    lax.fori_loop(0, GROUP, back_arrive, 0)
    first = (my_column == 0).astype(F32)

    def finish(h, carry):
        cut = pl.ds(pl.multiple_of(h * HEAD, HEAD), HEAD)
        state = CR[h].reshape(HEAD, HEAD)
        mixed = MIX[h] + first * jnp.dot(Q[:, cut], state, preferred_element_type=F32)
        scale = lax.rsqrt(jnp.mean(mixed * mixed, axis=-1, keepdims=True) + 1e-06)
        out[:, cut] = (mixed * scale * G[:, cut]).astype(BF16)
        return carry

    lax.fori_loop(0, 4, finish, 0)

    @pl.when(seq != c)
    def _():
        back_copy(0).wait_send()

    lax.fori_loop(1, GROUP, back_wait, 0)


def on_device(tokens, queries, flags, w_key, w_value, norm_gain):
    count, width = queries.shape[1:]
    dma = pltpu.SemaphoreType.DMA
    any_spec = pl.BlockSpec(memory_space=pltpu.HBM)
    vmem_spec = pl.BlockSpec(memory_space=pltpu.VMEM)
    attended = pl.pallas_call(
        kernel,
        out_shape=jax.ShapeDtypeStruct((count, width), BF16),
        in_specs=[any_spec] * 6,
        out_specs=vmem_spec,
        scratch_shapes=[
            pltpu.VMEM((2, count, tokens.shape[2]), BF16),
            pltpu.VMEM((count, width), BF16),
            pltpu.VMEM((2, 1, count), jnp.int32),
            pltpu.VMEM((1, width), F32),
            pltpu.VMEM((2, 2, 8, width), BF16),
            pltpu.VMEM((2, NX, NZ, NY, 16, 2 * HEAD), BF16),
            pltpu.VMEM((2, 2 * count, 2 * HEAD), F32),
            pltpu.VMEM((2, 4, 2, count, HEAD), BF16),
            pltpu.VMEM((2, HEAD, HEAD), F32),
            pltpu.VMEM((8, HEAD), F32),
            pltpu.VMEM((GROUP, 8, HEAD), F32),
            pltpu.VMEM((GROUP, HEAD // 4, HEAD), BF16),
            pltpu.VMEM((GROUP, HEAD // 4, HEAD), BF16),
            pltpu.VMEM((GROUP, HEAD // 4, HEAD), BF16),
            pltpu.VMEM((4, 4, HEAD // 4, HEAD), BF16),
            pltpu.VMEM((4, count, HEAD), F32),
            dma((6,)),
            dma((4,)),
            dma((4,)),
            dma((3,)),
            dma((3,)),
            dma((4, 4)),
            dma((4, 4)),
            dma((GROUP,)),
            dma((GROUP,)),
            dma((4, 2, 4)),
            dma((4, 2, 4)),
            dma((4, 2, 4)),
            dma((4, 2, 4)),
            dma((GROUP,)),
            dma((GROUP,)),
            dma((GROUP,)),
            dma((GROUP,)),
        ],
        compiler_params=pltpu.CompilerParams(
            collective_id=0, has_side_effects=True, vmem_limit_bytes=62 << 20
        ),
        name="attention",
    )(tokens[0], queries[0], flags, w_key, w_value, norm_gain.reshape(1, width))
    return attended.reshape(1, count, width)


def solution(mesh):
    in_specs = (
        P("fsdp", "ctx", None),
        P("fsdp", "ctx", None),
        P("fsdp", "ctx"),
        P(("ctx", "fsdp"), None),
        P(("ctx", "fsdp"), None),
        P(),
    )
    out_specs = P("fsdp", "ctx", None)
    return jax.shard_map(
        on_device, mesh=mesh, in_specs=in_specs, out_specs=out_specs, check_vma=False
    )
```

```python
import functools

import jax
import jax.numpy as jnp
from jax import lax
from jax.experimental import pallas as pl
from jax.experimental.pallas import tpu as pltpu
from jax.sharding import PartitionSpec as P

HEAD = 128
MESH = pl.DeviceIdType.MESH
NX, NY, NZ = 4, 4, 16
GROUP = 16
F32, BF16 = jnp.float32, jnp.bfloat16


def device(x, z, y, c):
    return (x * NZ + z, y * 2 + c)


def phi(u):
    return jnp.where(u > 0, u + 1.0, jnp.exp(jnp.minimum(u, 0.0)))


def segments(marks):
    n = marks.shape[1]
    t = lax.broadcasted_iota(jnp.int32, (n, n), 0)
    s = lax.broadcasted_iota(jnp.int32, (n, n), 1)
    wide = jnp.broadcast_to(marks, (n, n)).astype(F32)
    column = jnp.sum(jnp.where(s <= t, wide, 0.0), axis=1, keepdims=True)
    upright = jnp.sum(jnp.where(s == t, wide, 0.0), axis=1, keepdims=True)
    row = jnp.sum(jnp.where(t <= s, jnp.broadcast_to(upright, (n, n)), 0.0), axis=0, keepdims=True)
    last = jnp.sum(marks.astype(F32), axis=1, keepdims=True)
    return column, row, last


def kernel(
    tok, qry, flg, wk, wv, gain, out,
    T, Q, F, G, WB, W, acc, KV, TL, KG, ST, SR, CS, CR, MIX,
    loc, pair_s, pair_r, hop_s, hop_r, z_s, z_r, k_s, k_r, two_s, two_r, three_s, three_r, s1_s, s1_r, s2_s, s2_r,
):
    ctx, fsdp = lax.axis_index("ctx"), lax.axis_index("fsdp")
    x, z = ctx // NZ, lax.rem(ctx, NZ)
    y, c = fsdp // 2, lax.rem(fsdp, 2)
    quad, low = z // 4, lax.rem(z, 4)
    other = 1 - c
    sibling = device(x, z, y, other)

    def at_x(d):
        return device(lax.rem(x + d, NX), z, y, c)

    def at_y(d):
        return device(x, z, lax.rem(y + d, NY), c)

    def at_z(d):
        return device(x, lax.rem(z + d, NZ), y, c)

    def in_quad(d):
        return device(x, quad * 4 + lax.rem(low + d, 4), y, c)

    loads = [
        pltpu.make_async_copy(wk, WB.at[c, 0], loc.at[0]),
        pltpu.make_async_copy(wv, WB.at[c, 1], loc.at[1]),
        pltpu.make_async_copy(flg, F.at[c], loc.at[2]),
        pltpu.make_async_copy(tok, T.at[c], loc.at[3]),
        pltpu.make_async_copy(qry, Q, loc.at[4]),
        pltpu.make_async_copy(gain, G, loc.at[5]),
    ]
    for load in loads:
        load.start()

    barrier = pltpu.get_barrier_semaphore()

    def greet(to):
        pl.semaphore_signal(barrier, inc=1, device_id=to, device_id_type=MESH)

    def greet_xy(d, carry):
        greet(at_x(d))
        greet(at_y(d))
        greet(in_quad(d))
        return carry

    lax.fori_loop(1, 4, greet_xy, 0)
    greet(sibling)
    greet(at_z(4))
    greet(at_z(12))
    for load in loads[:3]:
        load.wait()
    pl.semaphore_wait(barrier, 12)

    def send(src, dst, ss, rs, to):
        return pltpu.make_async_remote_copy(
            src_ref=src, dst_ref=dst, send_sem=ss, recv_sem=rs, device_id=to, device_id_type=MESH
        )

    def same(ref, ss, rs, to):
        return send(ref, ref, ss, rs, to)

    def start(copies):
        for copy in copies:
            copy.start()

    def arrive(copies):
        for copy in copies:
            copy.wait_recv()

    swap_w = same(WB.at[c], pair_s.at[0], pair_r.at[0], sibling)
    swap_f = same(F.at[c], pair_s.at[1], pair_r.at[1], sibling)
    swap_t = same(T.at[c], pair_s.at[2], pair_r.at[2], sibling)
    start([swap_w, swap_f])
    arrive([swap_w])
    both = jnp.concatenate([WB[0].astype(F32), WB[1].astype(F32)], axis=1)
    mine = jnp.where(c == 0, both[:, :, : 2 * HEAD], both[:, :, 2 * HEAD :]).astype(BF16)
    for h in range(2):
        cut = slice(h * HEAD, (h + 1) * HEAD)
        W[h, x, z, y] = jnp.concatenate([mine[0, :, cut], mine[1, :, cut]], axis=1)

    def four(r):
        return pl.ds(lax.rem(quad + r, 4) * 4, 4)

    def hop(d, ahead, k):
        piece = W.at[:, x, lax.rem(z + ahead, NZ), y]
        return same(piece, hop_s.at[k], hop_r.at[k], at_z(d))

    hops = [hop(4, 0, 0), hop(12, 0, 1), hop(12, 4, 2)]

    def share(r):
        piece = W.at[:, x, lax.rem(z + 4 * r, NZ), y]
        return [same(piece, z_s.at[r, d], z_r.at[r, d], in_quad(d)) for d in range(1, 4)]

    def two(r):
        a, b = W.at[0, x, four(r), y], W.at[1, x, four(r), y]
        return [same(a, two_s.at[r, 0, d], two_r.at[r, 0, d], at_y(d)) for d in (1, 3, 2)] + [
            same(b, two_s.at[r, 1, d], two_r.at[r, 1, d], at_x(d)) for d in (1, 3, 2)
        ]

    def three(r):
        a, b = W.at[0, x, four(r)], W.at[1, :, four(r), y]
        return [same(a, three_s.at[r, 0, d], three_r.at[r, 0, d], at_x(d)) for d in (1, 3)] + [
            same(b, three_s.at[r, 1, d], three_r.at[r, 1, d], at_y(d)) for d in (1, 3)
        ]

    def far(r):
        to = jnp.where(lax.rem(r, 2) == 0, 1, 3)
        a = W.at[0, lax.rem(x + 4 - to, NX), four(r)]
        b = W.at[1, :, four(r), lax.rem(y + 4 - to, NY)]
        return [
            same(a, three_s.at[r, 0, 2], three_r.at[r, 0, 2], at_x(to)),
            same(b, three_s.at[r, 1, 2], three_r.at[r, 1, 2], at_y(to)),
        ]

    depth = 4 * NY * 16

    def project(h, part, r):
        q = lax.rem(quad + r, 4)
        cols = pl.ds(pl.multiple_of((part * 4 + q) * depth, depth), depth)
        rows = T[:, :, cols].reshape(2 * HEAD, depth)
        acc[h] += jnp.dot(
            rows, W[h, part, four(r)].reshape(depth, 2 * HEAD), preferred_element_type=F32
        )

    def near_a(r):
        def one(i, carry):
            project(0, lax.rem(x + 3 + i, NX), r)
            return carry

        lax.fori_loop(0, 3, one, 0)

    def rest(r):
        project(0, lax.rem(x + 2, NX), r)

        def one(i, carry):
            project(1, i, r)
            return carry

        lax.fori_loop(0, NX, one, 0)

    place = lax.rem(z + NZ // 2, GROUP)
    base = lax.rem(x + NX - jnp.where(place < GROUP // 2, 0, 1), NX)

    def member_x(p):
        return lax.rem(base + p // (GROUP // 2), NX)

    def member_z(p):
        return lax.rem(p + NZ // 2, NZ)

    def member(p, core):
        return device(member_x(p), member_z(p), y, core)

    def keep_four(r):
        return KG.at[x, four(r)]

    keep_in = [same(KG.at[x, z], k_s.at[d], k_r.at[d], in_quad(d)) for d in range(1, 4)]
    keep_z = [
        same(keep_four(0), k_s.at[4], k_r.at[4], at_z(4)),
        same(keep_four(0), k_s.at[5], k_r.at[5], at_z(12)),
    ]
    keep_far = [same(keep_four(1), k_s.at[6], k_r.at[6], at_z(12))]
    keep_x = [same(KG.at[x], k_s.at[6 + d], k_r.at[6 + d], at_x(d)) for d in (1, 3)]
    keep_all = keep_in + keep_z + keep_far + keep_x

    start(hops[:2])
    start(share(0))
    loads[3].wait()
    start([swap_t])
    arrive([swap_f])
    column, row, last = [], [], []
    for s in range(2):
        a, b, l = segments(F[s])
        column.append(a)
        row.append(b)
        last.append(l)
    keeps = [jnp.broadcast_to(jnp.where(l > 0, 0.0, 1.0), (4, HEAD)) for l in last]
    KG[x, z] = jnp.concatenate(keeps, axis=0)
    start(keep_in)
    acc[...] = jnp.zeros_like(acc)

    arrive(share(0))
    start(two(0))
    arrive(hops[:2])
    start(hops[2:])
    start(share(1))
    start(share(3))
    arrive(two(0))
    start(three(0))
    arrive(keep_in)
    start(keep_z)
    arrive(hops[2:])
    start(share(2))
    arrive(share(1))
    start(two(1))
    arrive(share(3))
    start(two(3))
    arrive(three(0))
    start(far(0))
    arrive(share(2))
    start(two(2))
    arrive(keep_z)
    start(keep_far)
    arrive(two(1))
    start(three(1))
    arrive(two(3))
    start(three(3))
    arrive([swap_t])
    near_a(0)
    arrive(far(0))
    rest(0)
    arrive(two(2))
    start(three(2))
    arrive(three(1))
    start(far(1))
    arrive(three(3))
    start(far(3))
    arrive(keep_far)
    start(keep_x)
    near_a(1)
    near_a(3)
    arrive(three(2))
    start(far(2))
    arrive(far(1))
    rest(1)
    arrive(far(3))
    rest(3)
    near_a(2)
    arrive(far(2))
    rest(2)

    def distant(i):
        step = (i + 1) // 2
        return jnp.where(lax.rem(i, 2) == 1, GROUP // 2 - step, GROUP // 2 + step)

    def one_copy(d):
        p = lax.rem(place + d, GROUP)
        return send(ST.at[p], SR.at[place], s1_s.at[d], s1_r.at[d], member(p, c))

    def one_start(d, carry):
        one_copy(distant(d)).start()
        return carry

    def one_wait(d, carry):
        one_copy(d).wait()
        return carry

    for s in range(2):
        TL[s] = jnp.broadcast_to((column[s] == last[s]).astype(F32), (HEAD, HEAD))

    def states(i, carry):
        s, h = i // 2, lax.rem(i, 2)
        part = acc[h, pl.ds(pl.multiple_of(s * HEAD, HEAD), HEAD), :]
        key = phi(part[:, :HEAD]).astype(BF16)
        value = part[:, HEAD:].astype(BF16)
        KV[s, 2 * c + h, 0] = key
        KV[s, 2 * c + h, 1] = value
        masked = (key.astype(F32) * TL[s]).astype(BF16)
        state = lax.dot_general(masked, value, (((0,), (0,)), ((), ())), preferred_element_type=F32)
        ST[pl.ds(4 * i, 4)] = state.astype(BF16).reshape(4, HEAD // 4, HEAD)
        return carry

    lax.fori_loop(0, 4, states, 0, unroll=True)
    lax.fori_loop(0, GROUP - 1, one_start, 0)
    SR[place] = ST[place]
    swap_kv = same(KV.at[other, pl.ds(2 * c, 2)], pair_s.at[3], pair_r.at[3], sibling)
    start([swap_kv])

    loads[4].wait()
    loads[5].wait()
    my_column = jnp.where(c == 0, column[0], column[1])
    my_row = jnp.where(c == 0, row[0], row[1])
    t = lax.broadcasted_iota(jnp.int32, (HEAD, HEAD), 0)
    u = lax.broadcasted_iota(jnp.int32, (HEAD, HEAD), 1)
    allowed = (u <= t) & (my_column == my_row)
    Q[...] = phi(Q[...].astype(F32)).astype(BF16)
    arrive([swap_kv])
    mask = allowed.astype(F32)

    def inside(h, carry):
        query = Q[:, pl.ds(pl.multiple_of(h * HEAD, HEAD), HEAD)]
        key, value = KV[c, h, 0], KV[c, h, 1]
        scores = lax.dot_general(query, key, (((1,), (1,)), ((), ())), preferred_element_type=F32)
        scores = (scores * mask).astype(BF16)
        MIX[h] = jnp.dot(scores, value, preferred_element_type=F32)
        return carry

    lax.fori_loop(0, 4, inside, 0, unroll=True)
    lax.fori_loop(1, GROUP, one_wait, 0)
    arrive(keep_x)
    seq = place // (GROUP // 2)

    def prefix(b, carried):
        CS[b] = carried.astype(BF16)
        tile = KG[member_x(b), member_z(b)]
        keep = jnp.where(seq == 0, tile[0:1], tile[4:5])
        return keep * carried + SR[b].astype(F32)

    lax.fori_loop(0, GROUP, prefix, jnp.zeros((HEAD // 4, HEAD), F32))

    mine_at = lax.rem(place, GROUP // 2)
    target = CR.at[2 * c + mine_at // 4, lax.rem(mine_at, 4)]
    index = c * 8 + mine_at

    def back_copy(d):
        p = lax.rem(place + d, GROUP)
        return send(CS.at[p], target, s2_s.at[d], s2_r.at[index], member(p, seq))

    def back_start(d, carry):
        back_copy(distant(d)).start()
        return carry

    def back_wait(d, carry):
        back_copy(d).wait_send()
        return carry

    own = pltpu.make_async_copy(CS.at[place], target, s2_r.at[index])

    lax.fori_loop(0, GROUP - 1, back_start, 0)

    @pl.when(seq == c)
    def _():
        own.start()

    @pl.when(seq != c)
    def _():
        back_copy(0).start()

    def back_arrive(i, carry):
        send(CS.at[0], CR.at[i // 4, lax.rem(i, 4)], s2_s.at[0], s2_r.at[i], sibling).wait_recv()
        return carry

    def drain(r, carry):
        for copy in share(r) + two(r) + three(r) + far(r):
            copy.wait_send()
        return carry

    lax.fori_loop(0, 4, drain, 0)
    for copy in hops + keep_all + [swap_w, swap_f, swap_t, swap_kv]:
        copy.wait_send()
    lax.fori_loop(0, GROUP, back_arrive, 0)
    first = (my_column == 0).astype(F32)

    def finish(h, carry):
        cut = pl.ds(pl.multiple_of(h * HEAD, HEAD), HEAD)
        state = CR[h].reshape(HEAD, HEAD)
        mixed = MIX[h] + first * jnp.dot(Q[:, cut], state, preferred_element_type=F32)
        scale = lax.rsqrt(jnp.mean(mixed * mixed, axis=-1, keepdims=True) + 1e-06)
        out[:, cut] = (mixed * scale * G[:, cut]).astype(BF16)
        return carry

    lax.fori_loop(0, 4, finish, 0, unroll=True)

    @pl.when(seq != c)
    def _():
        back_copy(0).wait_send()

    lax.fori_loop(1, GROUP, back_wait, 0)


def on_device(tokens, queries, flags, w_key, w_value, norm_gain):
    count, width = queries.shape[1:]
    dma = pltpu.SemaphoreType.DMA
    any_spec = pl.BlockSpec(memory_space=pltpu.HBM)
    vmem_spec = pl.BlockSpec(memory_space=pltpu.VMEM)
    attended = pl.pallas_call(
        kernel,
        out_shape=jax.ShapeDtypeStruct((count, width), BF16),
        in_specs=[any_spec] * 6,
        out_specs=vmem_spec,
        scratch_shapes=[
            pltpu.VMEM((2, count, tokens.shape[2]), BF16),
            pltpu.VMEM((count, width), BF16),
            pltpu.VMEM((2, 1, count), jnp.int32),
            pltpu.VMEM((1, width), F32),
            pltpu.VMEM((2, 2, 8, width), BF16),
            pltpu.VMEM((2, NX, NZ, NY, 16, 2 * HEAD), BF16),
            pltpu.VMEM((2, 2 * count, 2 * HEAD), F32),
            pltpu.VMEM((2, 4, 2, count, HEAD), BF16),
            pltpu.VMEM((2, HEAD, HEAD), F32),
            pltpu.VMEM((NX, NZ, 8, HEAD), F32),
            pltpu.VMEM((GROUP, HEAD // 4, HEAD), BF16),
            pltpu.VMEM((GROUP, HEAD // 4, HEAD), BF16),
            pltpu.VMEM((GROUP, HEAD // 4, HEAD), BF16),
            pltpu.VMEM((4, 4, HEAD // 4, HEAD), BF16),
            pltpu.VMEM((4, count, HEAD), F32),
            dma((6,)),
            dma((4,)),
            dma((4,)),
            dma((3,)),
            dma((3,)),
            dma((4, 4)),
            dma((4, 4)),
            dma((10,)),
            dma((10,)),
            dma((4, 2, 4)),
            dma((4, 2, 4)),
            dma((4, 2, 4)),
            dma((4, 2, 4)),
            dma((GROUP,)),
            dma((GROUP,)),
            dma((GROUP,)),
            dma((GROUP,)),
        ],
        compiler_params=pltpu.CompilerParams(
            collective_id=0, has_side_effects=True, vmem_limit_bytes=62 << 20
        ),
        name="attention",
    )(tokens[0], queries[0], flags, w_key, w_value, norm_gain.reshape(1, width))
    return attended.reshape(1, count, width)


def solution(mesh):
    in_specs = (
        P("fsdp", "ctx", None),
        P("fsdp", "ctx", None),
        P("fsdp", "ctx"),
        P(("ctx", "fsdp"), None),
        P(("ctx", "fsdp"), None),
        P(),
    )
    out_specs = P("fsdp", "ctx", None)
    return jax.shard_map(
        on_device, mesh=mesh, in_specs=in_specs, out_specs=out_specs, check_vma=False
    )
```

```python
import functools

import jax
import jax.numpy as jnp
from jax import lax
from jax.experimental import pallas as pl
from jax.experimental.pallas import tpu as pltpu
from jax.sharding import PartitionSpec as P

HEAD = 128
MESH = pl.DeviceIdType.MESH
NX, NY, NZ = 4, 4, 16
GROUP = 16
F32, BF16 = jnp.float32, jnp.bfloat16


def device(x, z, y, c):
    return (x * NZ + z, y * 2 + c)


def phi(u):
    return jnp.where(u > 0, u + 1.0, jnp.exp(jnp.minimum(u, 0.0)))


def segments(marks):
    n = marks.shape[1]
    t = lax.broadcasted_iota(jnp.int32, (n, n), 0)
    s = lax.broadcasted_iota(jnp.int32, (n, n), 1)
    wide = jnp.broadcast_to(marks, (n, n)).astype(F32)
    column = jnp.sum(jnp.where(s <= t, wide, 0.0), axis=1, keepdims=True)
    upright = jnp.sum(jnp.where(s == t, wide, 0.0), axis=1, keepdims=True)
    row = jnp.sum(jnp.where(t <= s, jnp.broadcast_to(upright, (n, n)), 0.0), axis=0, keepdims=True)
    last = jnp.sum(marks.astype(F32), axis=1, keepdims=True)
    return column, row, last


def kernel(
    tok, qry, flg, wk, wv, gain, out,
    T, Q, F, G, WB, W, acc, KV, TL, KG, ST, SR, CS, CR, MIX,
    loc, pair_s, pair_r, hop_s, hop_r, z_s, z_r, k_s, k_r, two_s, two_r, three_s, three_r, s1_s, s1_r, s2_s, s2_r,
):
    ctx, fsdp = lax.axis_index("ctx"), lax.axis_index("fsdp")
    x, z = ctx // NZ, lax.rem(ctx, NZ)
    y, c = fsdp // 2, lax.rem(fsdp, 2)
    quad, low = z // 4, lax.rem(z, 4)
    other = 1 - c
    sibling = device(x, z, y, other)

    def at_x(d):
        return device(lax.rem(x + d, NX), z, y, c)

    def at_y(d):
        return device(x, z, lax.rem(y + d, NY), c)

    def at_z(d):
        return device(x, lax.rem(z + d, NZ), y, c)

    def in_quad(d):
        return device(x, quad * 4 + lax.rem(low + d, 4), y, c)

    loads = [
        pltpu.make_async_copy(wk, WB.at[c, 0], loc.at[0]),
        pltpu.make_async_copy(wv, WB.at[c, 1], loc.at[1]),
        pltpu.make_async_copy(flg, F.at[c], loc.at[2]),
        pltpu.make_async_copy(tok, T.at[c], loc.at[3]),
        pltpu.make_async_copy(qry, Q, loc.at[4]),
        pltpu.make_async_copy(gain, G, loc.at[5]),
    ]

    barrier = pltpu.get_barrier_semaphore()

    def greet(to):
        pl.semaphore_signal(barrier, inc=1, device_id=to, device_id_type=MESH)

    def greet_xy(d, carry):
        greet(at_x(d))
        greet(at_y(d))
        greet(in_quad(d))
        return carry

    greet(at_z(4))
    greet(at_z(12))
    lax.fori_loop(1, 4, greet_xy, 0, unroll=True)
    greet(sibling)
    for load in loads:
        load.start()
    for load in loads[:3]:
        load.wait()
    pl.semaphore_wait(barrier, 12)

    def send(src, dst, ss, rs, to):
        return pltpu.make_async_remote_copy(
            src_ref=src, dst_ref=dst, send_sem=ss, recv_sem=rs, device_id=to, device_id_type=MESH
        )

    def same(ref, ss, rs, to):
        return send(ref, ref, ss, rs, to)

    def start(copies):
        for copy in copies:
            copy.start()

    def arrive(copies):
        for copy in copies:
            copy.wait_recv()

    swap_w = same(WB.at[c], pair_s.at[0], pair_r.at[0], sibling)
    swap_f = same(F.at[c], pair_s.at[1], pair_r.at[1], sibling)
    swap_t = same(T.at[c], pair_s.at[2], pair_r.at[2], sibling)
    start([swap_w, swap_f])
    arrive([swap_w])
    both = jnp.concatenate([WB[0].astype(F32), WB[1].astype(F32)], axis=1)
    mine = jnp.where(c == 0, both[:, :, : 2 * HEAD], both[:, :, 2 * HEAD :]).astype(BF16)
    for h in range(2):
        cut = slice(h * HEAD, (h + 1) * HEAD)
        W[h, x, z, y] = jnp.concatenate([mine[0, :, cut], mine[1, :, cut]], axis=1)

    def four(r):
        return pl.ds(lax.rem(quad + r, 4) * 4, 4)

    def hop(d, ahead, k):
        piece = W.at[:, x, lax.rem(z + ahead, NZ), y]
        return same(piece, hop_s.at[k], hop_r.at[k], at_z(d))

    hops = [hop(4, 0, 0), hop(12, 0, 1), hop(12, 4, 2)]

    def share(r):
        piece = W.at[:, x, lax.rem(z + 4 * r, NZ), y]
        return [same(piece, z_s.at[r, d], z_r.at[r, d], in_quad(d)) for d in range(1, 4)]

    def two(r):
        a, b = W.at[0, x, four(r), y], W.at[1, x, four(r), y]
        return [same(a, two_s.at[r, 0, d], two_r.at[r, 0, d], at_y(d)) for d in (1, 3, 2)] + [
            same(b, two_s.at[r, 1, d], two_r.at[r, 1, d], at_x(d)) for d in (1, 3, 2)
        ]

    def three(r):
        a, b = W.at[0, x, four(r)], W.at[1, :, four(r), y]
        return [same(a, three_s.at[r, 0, d], three_r.at[r, 0, d], at_x(d)) for d in (1, 3)] + [
            same(b, three_s.at[r, 1, d], three_r.at[r, 1, d], at_y(d)) for d in (1, 3)
        ]

    def far(r):
        copies = []
        for side, (to, back) in enumerate(((1, 3), (3, 1))):
            part = pl.ds(lax.rem(quad + r, 4) * 4 + 2 * side, 2)
            a = W.at[0, lax.rem(x + back, NX), part]
            b = W.at[1, :, part, lax.rem(y + back, NY)]
            k = 2 - 2 * side
            copies += [
                same(a, three_s.at[r, 0, k], three_r.at[r, 0, k], at_x(to)),
                same(b, three_s.at[r, 1, k], three_r.at[r, 1, k], at_y(to)),
            ]
        return copies

    depth = 4 * NY * 16

    def project(h, part, r):
        q = lax.rem(quad + r, 4)
        cols = pl.ds(pl.multiple_of((part * 4 + q) * depth, depth), depth)
        rows = T[:, :, cols].reshape(2 * HEAD, depth)
        acc[h] += jnp.dot(
            rows, W[h, part, four(r)].reshape(depth, 2 * HEAD), preferred_element_type=F32
        )

    def near_a(r):
        q = lax.rem(quad + r, 4)
        parts = [lax.rem(x + 3 + i, NX) for i in range(3)]
        rows = jnp.concatenate(
            [T[:, :, pl.ds(pl.multiple_of((i * 4 + q) * depth, depth), depth)] for i in parts], axis=2
        )
        sides = jnp.concatenate([W[0, i, four(r)].reshape(depth, 2 * HEAD) for i in parts], axis=0)
        acc[0] += jnp.dot(rows.reshape(2 * HEAD, 3 * depth), sides, preferred_element_type=F32)

    def rest(r):
        project(0, lax.rem(x + 2, NX), r)
        q = lax.rem(quad + r, 4)
        rows = jnp.concatenate(
            [T[:, :, pl.ds(pl.multiple_of((i * 4 + q) * depth, depth), depth)] for i in range(NX)], axis=2
        )
        acc[1] += jnp.dot(
            rows.reshape(2 * HEAD, NX * depth),
            W[1, :, four(r)].reshape(NX * depth, 2 * HEAD),
            preferred_element_type=F32,
        )

    place = lax.rem(z + NZ // 2, GROUP)
    base = lax.rem(x + NX - jnp.where(place < GROUP // 2, 0, 1), NX)

    def member_x(p):
        return lax.rem(base + p // (GROUP // 2), NX)

    def member_z(p):
        return lax.rem(p + NZ // 2, NZ)

    def member(p, core):
        return device(member_x(p), member_z(p), y, core)

    def keep_four(r):
        return KG.at[x, four(r)]

    keep_in = [same(KG.at[x, z], k_s.at[d], k_r.at[d], in_quad(d)) for d in range(1, 4)]
    keep_z = [
        same(keep_four(0), k_s.at[4], k_r.at[4], at_z(4)),
        same(keep_four(0), k_s.at[5], k_r.at[5], at_z(12)),
    ]
    keep_far = [same(keep_four(1), k_s.at[6], k_r.at[6], at_z(12))]
    keep_x = [same(KG.at[x], k_s.at[6 + d], k_r.at[6 + d], at_x(d)) for d in (1, 3)]
    keep_all = keep_in + keep_z + keep_far + keep_x

    start(hops[:2])
    start(share(0))
    loads[3].wait()
    start([swap_t])
    arrive([swap_f])
    column, row, last = [], [], []
    for s in range(2):
        a, b, l = segments(F[s])
        column.append(a)
        row.append(b)
        last.append(l)
    keeps = [jnp.broadcast_to(jnp.where(l > 0, 0.0, 1.0), (4, HEAD)) for l in last]
    KG[x, z] = jnp.concatenate(keeps, axis=0)
    start(keep_in)
    acc[...] = jnp.zeros_like(acc)

    arrive(share(0))
    start(two(0))
    arrive(hops[:2])
    start(hops[2:])
    start(share(1))
    start(share(3))
    arrive(two(0))
    start(three(0))
    arrive(keep_in)
    start(keep_z)
    arrive(hops[2:])
    start(share(2))
    arrive(share(1))
    start(two(1))
    arrive(share(3))
    start(two(3))
    arrive(three(0))
    start(far(0))
    arrive(share(2))
    start(two(2))
    arrive(keep_z)
    start(keep_far)
    arrive(two(1))
    start(three(1))
    arrive(two(3))
    start(three(3))
    arrive([swap_t])
    near_a(0)
    arrive(far(0))
    rest(0)
    arrive(two(2))
    start(three(2))
    arrive(three(1))
    start(far(1))
    arrive(three(3))
    start(far(3))
    arrive(keep_far)
    start(keep_x)
    near, ahead = three(2), far(2)
    arrive([near[0], near[2]])
    start(ahead[:2])
    arrive([near[1], near[3]])
    start(ahead[2:])
    near_a(1)
    near_a(3)
    arrive(far(1))
    rest(1)
    arrive(far(3))
    rest(3)
    near_a(2)
    arrive(far(2))
    rest(2)

    def distant(i):
        step = (i + 1) // 2
        return jnp.where(lax.rem(i, 2) == 1, GROUP // 2 - step, GROUP // 2 + step)

    def one_copy(d):
        p = lax.rem(place + d, GROUP)
        return send(ST.at[p], SR.at[place], s1_s.at[d], s1_r.at[d], member(p, c))

    def one_start(d, carry):
        one_copy(distant(d)).start()
        return carry

    def one_wait(d, carry):
        one_copy(d).wait()
        return carry

    for s in range(2):
        TL[s] = jnp.broadcast_to((column[s] == last[s]).astype(F32), (HEAD, HEAD))

    def states(i, carry):
        s, h = i // 2, lax.rem(i, 2)
        part = acc[h, pl.ds(pl.multiple_of(s * HEAD, HEAD), HEAD), :]
        key = phi(part[:, :HEAD]).astype(BF16)
        value = part[:, HEAD:].astype(BF16)
        KV[s, 2 * c + h, 0] = key
        KV[s, 2 * c + h, 1] = value
        masked = (key.astype(F32) * TL[s]).astype(BF16)
        state = lax.dot_general(masked, value, (((0,), (0,)), ((), ())), preferred_element_type=F32)
        ST[pl.ds(4 * i, 4)] = state.astype(BF16).reshape(4, HEAD // 4, HEAD)
        return carry

    lax.fori_loop(0, 4, states, 0, unroll=True)
    lax.fori_loop(0, GROUP - 1, one_start, 0, unroll=True)
    SR[place] = ST[place]
    swap_kv = same(KV.at[other, pl.ds(2 * c, 2)], pair_s.at[3], pair_r.at[3], sibling)
    start([swap_kv])

    loads[4].wait()
    loads[5].wait()
    my_column = jnp.where(c == 0, column[0], column[1])
    my_row = jnp.where(c == 0, row[0], row[1])
    t = lax.broadcasted_iota(jnp.int32, (HEAD, HEAD), 0)
    u = lax.broadcasted_iota(jnp.int32, (HEAD, HEAD), 1)
    allowed = (u <= t) & (my_column == my_row)
    Q[...] = phi(Q[...].astype(F32)).astype(BF16)
    arrive([swap_kv])
    mask = allowed.astype(F32)

    def inside(h, carry):
        query = Q[:, pl.ds(pl.multiple_of(h * HEAD, HEAD), HEAD)]
        key, value = KV[c, h, 0], KV[c, h, 1]
        scores = lax.dot_general(query, key, (((1,), (1,)), ((), ())), preferred_element_type=F32)
        scores = (scores * mask).astype(BF16)
        MIX[h] = jnp.dot(scores, value, preferred_element_type=F32)
        return carry

    lax.fori_loop(0, 4, inside, 0, unroll=True)
    lax.fori_loop(1, GROUP, one_wait, 0)
    arrive(keep_x)
    seq = place // (GROUP // 2)

    def prefix(b, carried):
        CS[b] = carried.astype(BF16)
        tile = KG[member_x(b), member_z(b)]
        keep = jnp.where(seq == 0, tile[0:1], tile[4:5])
        return keep * carried + SR[b].astype(F32)

    lax.fori_loop(0, GROUP, prefix, jnp.zeros((HEAD // 4, HEAD), F32))

    mine_at = lax.rem(place, GROUP // 2)
    target = CR.at[2 * c + mine_at // 4, lax.rem(mine_at, 4)]
    index = c * 8 + mine_at

    def back_copy(d):
        p = lax.rem(place + d, GROUP)
        return send(CS.at[p], target, s2_s.at[d], s2_r.at[index], member(p, seq))

    def back_start(d, carry):
        back_copy(distant(d)).start()
        return carry

    def back_wait(d, carry):
        back_copy(d).wait_send()
        return carry

    own = pltpu.make_async_copy(CS.at[place], target, s2_r.at[index])

    lax.fori_loop(0, GROUP - 1, back_start, 0, unroll=True)

    @pl.when(seq == c)
    def _():
        own.start()

    @pl.when(seq != c)
    def _():
        back_copy(0).start()

    def back_arrive(i, carry):
        send(CS.at[0], CR.at[i // 4, lax.rem(i, 4)], s2_s.at[0], s2_r.at[i], sibling).wait_recv()
        return carry

    def drain(r, carry):
        for copy in share(r) + two(r) + three(r) + far(r):
            copy.wait_send()
        return carry

    lax.fori_loop(0, 4, drain, 0)
    for copy in hops + keep_all + [swap_w, swap_f, swap_t, swap_kv]:
        copy.wait_send()
    lax.fori_loop(0, GROUP, back_arrive, 0)
    first = (my_column == 0).astype(F32)

    def finish(h, carry):
        cut = pl.ds(pl.multiple_of(h * HEAD, HEAD), HEAD)
        state = CR[h].reshape(HEAD, HEAD)
        mixed = MIX[h] + first * jnp.dot(Q[:, cut], state, preferred_element_type=F32)
        scale = lax.rsqrt(jnp.mean(mixed * mixed, axis=-1, keepdims=True) + 1e-06)
        out[:, cut] = (mixed * scale * G[:, cut]).astype(BF16)
        return carry

    lax.fori_loop(0, 4, finish, 0, unroll=True)

    @pl.when(seq != c)
    def _():
        back_copy(0).wait_send()

    lax.fori_loop(1, GROUP, back_wait, 0)


def on_device(tokens, queries, flags, w_key, w_value, norm_gain):
    count, width = queries.shape[1:]
    dma = pltpu.SemaphoreType.DMA
    any_spec = pl.BlockSpec(memory_space=pltpu.HBM)
    vmem_spec = pl.BlockSpec(memory_space=pltpu.VMEM)
    attended = pl.pallas_call(
        kernel,
        out_shape=jax.ShapeDtypeStruct((count, width), BF16),
        in_specs=[any_spec] * 6,
        out_specs=vmem_spec,
        scratch_shapes=[
            pltpu.VMEM((2, count, tokens.shape[2]), BF16),
            pltpu.VMEM((count, width), BF16),
            pltpu.VMEM((2, 1, count), jnp.int32),
            pltpu.VMEM((1, width), F32),
            pltpu.VMEM((2, 2, 8, width), BF16),
            pltpu.VMEM((2, NX, NZ, NY, 16, 2 * HEAD), BF16),
            pltpu.VMEM((2, 2 * count, 2 * HEAD), F32),
            pltpu.VMEM((2, 4, 2, count, HEAD), BF16),
            pltpu.VMEM((2, HEAD, HEAD), F32),
            pltpu.VMEM((NX, NZ, 8, HEAD), F32),
            pltpu.VMEM((GROUP, HEAD // 4, HEAD), BF16),
            pltpu.VMEM((GROUP, HEAD // 4, HEAD), BF16),
            pltpu.VMEM((GROUP, HEAD // 4, HEAD), BF16),
            pltpu.VMEM((4, 4, HEAD // 4, HEAD), BF16),
            pltpu.VMEM((4, count, HEAD), F32),
            dma((6,)),
            dma((4,)),
            dma((4,)),
            dma((3,)),
            dma((3,)),
            dma((4, 4)),
            dma((4, 4)),
            dma((10,)),
            dma((10,)),
            dma((4, 2, 4)),
            dma((4, 2, 4)),
            dma((4, 2, 4)),
            dma((4, 2, 4)),
            dma((GROUP,)),
            dma((GROUP,)),
            dma((GROUP,)),
            dma((GROUP,)),
        ],
        compiler_params=pltpu.CompilerParams(
            collective_id=0, has_side_effects=True, vmem_limit_bytes=62 << 20
        ),
        name="attention",
    )(tokens[0], queries[0], flags, w_key, w_value, norm_gain.reshape(1, width))
    return attended.reshape(1, count, width)


def solution(mesh):
    in_specs = (
        P("fsdp", "ctx", None),
        P("fsdp", "ctx", None),
        P("fsdp", "ctx"),
        P(("ctx", "fsdp"), None),
        P(("ctx", "fsdp"), None),
        P(),
    )
    out_specs = P("fsdp", "ctx", None)
    return jax.shard_map(
        on_device, mesh=mesh, in_specs=in_specs, out_specs=out_specs, check_vma=False
    )
```

```python
import functools

import jax
import jax.numpy as jnp
from jax import lax
from jax.experimental import pallas as pl
from jax.experimental.pallas import tpu as pltpu
from jax.sharding import PartitionSpec as P

HEAD = 128
MESH = pl.DeviceIdType.MESH
NX, NY, NZ = 4, 4, 16
GROUP = 16
F32, BF16 = jnp.float32, jnp.bfloat16


def device(x, z, y, c):
    return (x * NZ + z, y * 2 + c)


def phi(u):
    return jnp.where(u > 0, u + 1.0, jnp.exp(jnp.minimum(u, 0.0)))


def segments(marks):
    n = marks.shape[1]
    t = lax.broadcasted_iota(jnp.int32, (n, n), 0)
    s = lax.broadcasted_iota(jnp.int32, (n, n), 1)
    wide = jnp.broadcast_to(marks, (n, n)).astype(F32)
    column = jnp.sum(jnp.where(s <= t, wide, 0.0), axis=1, keepdims=True)
    upright = jnp.sum(jnp.where(s == t, wide, 0.0), axis=1, keepdims=True)
    row = jnp.sum(jnp.where(t <= s, jnp.broadcast_to(upright, (n, n)), 0.0), axis=0, keepdims=True)
    last = jnp.sum(marks.astype(F32), axis=1, keepdims=True)
    return column, row, last


def kernel(
    tok, qry, flg, wk, wv, gain, out,
    T, Q, F, G, WB, W, acc, KV, TL, KG, ST, SR, CS, CR, MIX,
    loc, pair_s, pair_r, hop_s, hop_r, z_s, z_r, k_s, k_r, two_s, two_r, three_s, three_r, s1_s, s1_r, s2_s, s2_r,
):
    ctx, fsdp = lax.axis_index("ctx"), lax.axis_index("fsdp")
    x, z = ctx // NZ, lax.rem(ctx, NZ)
    y, c = fsdp // 2, lax.rem(fsdp, 2)
    quad, low = z // 4, lax.rem(z, 4)
    other = 1 - c
    sibling = device(x, z, y, other)

    def at_x(d):
        return device(lax.rem(x + d, NX), z, y, c)

    def at_y(d):
        return device(x, z, lax.rem(y + d, NY), c)

    def at_z(d):
        return device(x, lax.rem(z + d, NZ), y, c)

    def in_quad(d):
        return device(x, quad * 4 + lax.rem(low + d, 4), y, c)

    loads = [
        pltpu.make_async_copy(wk, WB.at[c, 0], loc.at[0]),
        pltpu.make_async_copy(wv, WB.at[c, 1], loc.at[1]),
        pltpu.make_async_copy(flg, F.at[c], loc.at[2]),
        pltpu.make_async_copy(tok, T.at[c], loc.at[3]),
        pltpu.make_async_copy(qry, Q, loc.at[4]),
        pltpu.make_async_copy(gain, G, loc.at[5]),
    ]

    barrier = pltpu.get_barrier_semaphore()

    def greet(to):
        pl.semaphore_signal(barrier, inc=1, device_id=to, device_id_type=MESH)

    def greet_xy(d, carry):
        greet(at_x(d))
        greet(at_y(d))
        greet(in_quad(d))
        return carry

    greet(at_z(4))
    greet(at_z(12))
    lax.fori_loop(1, 4, greet_xy, 0, unroll=True)
    greet(sibling)
    for load in loads:
        load.start()
    for load in loads[:3]:
        load.wait()
    pl.semaphore_wait(barrier, 12)

    def send(src, dst, ss, rs, to):
        return pltpu.make_async_remote_copy(
            src_ref=src, dst_ref=dst, send_sem=ss, recv_sem=rs, device_id=to, device_id_type=MESH
        )

    def same(ref, ss, rs, to):
        return send(ref, ref, ss, rs, to)

    def start(copies):
        for copy in copies:
            copy.start()

    def arrive(copies):
        for copy in copies:
            copy.wait_recv()

    swap_w = same(WB.at[c], pair_s.at[0], pair_r.at[0], sibling)
    swap_f = same(F.at[c], pair_s.at[1], pair_r.at[1], sibling)
    swap_t = same(T.at[c], pair_s.at[2], pair_r.at[2], sibling)
    start([swap_w, swap_f])
    arrive([swap_w])
    both = jnp.concatenate([WB[0].astype(F32), WB[1].astype(F32)], axis=1)
    mine = jnp.where(c == 0, both[:, :, : 2 * HEAD], both[:, :, 2 * HEAD :]).astype(BF16)
    for h in range(2):
        cut = slice(h * HEAD, (h + 1) * HEAD)
        W[h, x, z, y] = jnp.concatenate([mine[0, :, cut], mine[1, :, cut]], axis=1)

    def four(r):
        return pl.ds(lax.rem(quad + r, 4) * 4, 4)

    def hop(d, ahead, k):
        piece = W.at[:, x, lax.rem(z + ahead, NZ), y]
        return same(piece, hop_s.at[k], hop_r.at[k], at_z(d))

    hops = [hop(4, 0, 0), hop(12, 0, 1), hop(12, 4, 2)]

    def share(r):
        piece = W.at[:, x, lax.rem(z + 4 * r, NZ), y]
        return [same(piece, z_s.at[r, d], z_r.at[r, d], in_quad(d)) for d in range(1, 4)]

    def two(r):
        a, b = W.at[0, x, four(r), y], W.at[1, x, four(r), y]
        return [same(a, two_s.at[r, 0, d], two_r.at[r, 0, d], at_y(d)) for d in (1, 3, 2)] + [
            same(b, two_s.at[r, 1, d], two_r.at[r, 1, d], at_x(d)) for d in (1, 3, 2)
        ]

    def three(r):
        a, b = W.at[0, x, four(r)], W.at[1, :, four(r), y]
        return [same(a, three_s.at[r, 0, d], three_r.at[r, 0, d], at_x(d)) for d in (1, 3)] + [
            same(b, three_s.at[r, 1, d], three_r.at[r, 1, d], at_y(d)) for d in (1, 3)
        ]

    def far(r):
        copies = []
        for side, (to, back) in enumerate(((1, 3), (3, 1))):
            part = pl.ds(lax.rem(quad + r, 4) * 4 + 2 * side, 2)
            a = W.at[0, lax.rem(x + back, NX), part]
            b = W.at[1, :, part, lax.rem(y + back, NY)]
            k = 2 - 2 * side
            copies += [
                same(a, three_s.at[r, 0, k], three_r.at[r, 0, k], at_x(to)),
                same(b, three_s.at[r, 1, k], three_r.at[r, 1, k], at_y(to)),
            ]
        return copies

    depth = 4 * NY * 16

    def project(h, part, r):
        q = lax.rem(quad + r, 4)
        cols = pl.ds(pl.multiple_of((part * 4 + q) * depth, depth), depth)
        rows = T[:, :, cols].reshape(2 * HEAD, depth)
        acc[h] += jnp.dot(
            rows, W[h, part, four(r)].reshape(depth, 2 * HEAD), preferred_element_type=F32
        )

    def near_a(r):
        q = lax.rem(quad + r, 4)
        parts = [lax.rem(x + 3 + i, NX) for i in range(3)]
        rows = jnp.concatenate(
            [T[:, :, pl.ds(pl.multiple_of((i * 4 + q) * depth, depth), depth)] for i in parts], axis=2
        )
        sides = jnp.concatenate([W[0, i, four(r)].reshape(depth, 2 * HEAD) for i in parts], axis=0)
        acc[0] += jnp.dot(rows.reshape(2 * HEAD, 3 * depth), sides, preferred_element_type=F32)

    def rest(r):
        project(0, lax.rem(x + 2, NX), r)
        q = lax.rem(quad + r, 4)
        rows = jnp.concatenate(
            [T[:, :, pl.ds(pl.multiple_of((i * 4 + q) * depth, depth), depth)] for i in range(NX)], axis=2
        )
        acc[1] += jnp.dot(
            rows.reshape(2 * HEAD, NX * depth),
            W[1, :, four(r)].reshape(NX * depth, 2 * HEAD),
            preferred_element_type=F32,
        )

    place = lax.rem(z + NZ // 2, GROUP)
    base = lax.rem(x + NX - jnp.where(place < GROUP // 2, 0, 1), NX)

    def member_x(p):
        return lax.rem(base + p // (GROUP // 2), NX)

    def member_z(p):
        return lax.rem(p + NZ // 2, NZ)

    def member(p, core):
        return device(member_x(p), member_z(p), y, core)

    def keep_four(r):
        return KG.at[x, four(r)]

    keep_in = [same(KG.at[x, z], k_s.at[d], k_r.at[d], in_quad(d)) for d in range(1, 4)]
    keep_z = [
        same(keep_four(0), k_s.at[4], k_r.at[4], at_z(4)),
        same(keep_four(0), k_s.at[5], k_r.at[5], at_z(12)),
    ]
    keep_far = [same(keep_four(1), k_s.at[6], k_r.at[6], at_z(12))]
    keep_x = [same(KG.at[x], k_s.at[6 + d], k_r.at[6 + d], at_x(d)) for d in (1, 3)]
    keep_all = keep_in + keep_z + keep_far + keep_x

    start(hops[:2])
    start(share(0))
    loads[3].wait()
    start([swap_t])
    arrive([swap_f])
    column, row, last = [], [], []
    for s in range(2):
        a, b, l = segments(F[s])
        column.append(a)
        row.append(b)
        last.append(l)
    keeps = [jnp.broadcast_to(jnp.where(l > 0, 0.0, 1.0), (4, HEAD)) for l in last]
    KG[x, z] = jnp.concatenate(keeps, axis=0)
    start(keep_in)
    acc[...] = jnp.zeros_like(acc)

    arrive(share(0))
    start(two(0))
    arrive([hops[1]])
    start(hops[2:])
    start(share(1))
    arrive([hops[0]])
    start(share(3))
    arrive(two(0))
    start(three(0))
    arrive(keep_in)
    start(keep_z)
    arrive(hops[2:])
    start(share(2))
    arrive(share(1))
    start(two(1))
    arrive(share(3))
    start(two(3))
    arrive(three(0))
    start(far(0))
    arrive(share(2))
    start(two(2))
    arrive(keep_z)
    start(keep_far)
    arrive(two(1))
    start(three(1))
    arrive(two(3))
    start(three(3))
    arrive([swap_t])
    near_a(0)
    arrive(far(0))
    rest(0)
    arrive(two(2))
    start(three(2))
    arrive(three(1))
    start(far(1))
    arrive(three(3))
    start(far(3))
    arrive(keep_far)
    start(keep_x)
    near, ahead = three(2), far(2)
    arrive([near[0], near[2]])
    start(ahead[:2])
    arrive([near[1], near[3]])
    start(ahead[2:])
    near_a(1)
    near_a(3)
    arrive(far(1))
    rest(1)
    arrive(far(3))
    rest(3)
    near_a(2)
    arrive(far(2))
    rest(2)

    def distant(i):
        step = (i + 1) // 2
        return jnp.where(lax.rem(i, 2) == 1, GROUP // 2 - step, GROUP // 2 + step)

    def one_copy(d):
        p = lax.rem(place + d, GROUP)
        return send(ST.at[p], SR.at[place], s1_s.at[d], s1_r.at[d], member(p, c))

    def one_start(d, carry):
        one_copy(distant(d)).start()
        return carry

    def one_wait(d, carry):
        one_copy(d).wait()
        return carry

    for s in range(2):
        TL[s] = jnp.broadcast_to((column[s] == last[s]).astype(F32), (HEAD, HEAD))

    def states(i, carry):
        s, h = i // 2, lax.rem(i, 2)
        part = acc[h, pl.ds(pl.multiple_of(s * HEAD, HEAD), HEAD), :]
        key = phi(part[:, :HEAD]).astype(BF16)
        value = part[:, HEAD:].astype(BF16)
        KV[s, 2 * c + h, 0] = key
        KV[s, 2 * c + h, 1] = value
        masked = (key.astype(F32) * TL[s]).astype(BF16)
        state = lax.dot_general(masked, value, (((0,), (0,)), ((), ())), preferred_element_type=F32)
        ST[pl.ds(4 * i, 4)] = state.astype(BF16).reshape(4, HEAD // 4, HEAD)
        return carry

    lax.fori_loop(0, 4, states, 0, unroll=True)
    lax.fori_loop(0, GROUP - 1, one_start, 0, unroll=True)
    SR[place] = ST[place]
    swap_kv = same(KV.at[other, pl.ds(2 * c, 2)], pair_s.at[3], pair_r.at[3], sibling)
    start([swap_kv])

    loads[4].wait()
    loads[5].wait()
    my_column = jnp.where(c == 0, column[0], column[1])
    my_row = jnp.where(c == 0, row[0], row[1])
    t = lax.broadcasted_iota(jnp.int32, (HEAD, HEAD), 0)
    u = lax.broadcasted_iota(jnp.int32, (HEAD, HEAD), 1)
    allowed = (u <= t) & (my_column == my_row)
    Q[...] = phi(Q[...].astype(F32)).astype(BF16)
    arrive([swap_kv])
    mask = allowed.astype(F32)

    def inside(h, carry):
        query = Q[:, pl.ds(pl.multiple_of(h * HEAD, HEAD), HEAD)]
        key, value = KV[c, h, 0], KV[c, h, 1]
        scores = lax.dot_general(query, key, (((1,), (1,)), ((), ())), preferred_element_type=F32)
        scores = (scores * mask).astype(BF16)
        MIX[h] = jnp.dot(scores, value, preferred_element_type=F32)
        return carry

    lax.fori_loop(0, 4, inside, 0, unroll=True)
    lax.fori_loop(1, GROUP, one_wait, 0)
    arrive(keep_x)
    seq = place // (GROUP // 2)

    def prefix(b, carried):
        CS[b] = carried.astype(BF16)
        tile = KG[member_x(b), member_z(b)]
        keep = jnp.where(seq == 0, tile[0:1], tile[4:5])
        return keep * carried + SR[b].astype(F32)

    lax.fori_loop(0, GROUP, prefix, jnp.zeros((HEAD // 4, HEAD), F32))

    mine_at = lax.rem(place, GROUP // 2)
    target = CR.at[2 * c + mine_at // 4, lax.rem(mine_at, 4)]
    index = c * 8 + mine_at

    def back_copy(d):
        p = lax.rem(place + d, GROUP)
        return send(CS.at[p], target, s2_s.at[d], s2_r.at[index], member(p, seq))

    def back_start(d, carry):
        back_copy(distant(d)).start()
        return carry

    def back_wait(d, carry):
        back_copy(d).wait_send()
        return carry

    own = pltpu.make_async_copy(CS.at[place], target, s2_r.at[index])

    lax.fori_loop(0, GROUP - 1, back_start, 0, unroll=True)

    @pl.when(seq == c)
    def _():
        own.start()

    @pl.when(seq != c)
    def _():
        back_copy(0).start()

    def back_arrive(i, carry):
        send(CS.at[0], CR.at[i // 4, lax.rem(i, 4)], s2_s.at[0], s2_r.at[i], sibling).wait_recv()
        return carry

    def drain(r, carry):
        for copy in share(r) + two(r) + three(r) + far(r):
            copy.wait_send()
        return carry

    lax.fori_loop(0, 4, drain, 0)
    for copy in hops + keep_all + [swap_w, swap_f, swap_t, swap_kv]:
        copy.wait_send()
    lax.fori_loop(0, GROUP, back_arrive, 0)
    first = (my_column == 0).astype(F32)

    def finish(h, carry):
        cut = pl.ds(pl.multiple_of(h * HEAD, HEAD), HEAD)
        state = CR[h].reshape(HEAD, HEAD)
        mixed = MIX[h] + first * jnp.dot(Q[:, cut], state, preferred_element_type=F32)
        scale = lax.rsqrt(jnp.mean(mixed * mixed, axis=-1, keepdims=True) + 1e-06)
        out[:, cut] = (mixed * scale * G[:, cut]).astype(BF16)
        return carry

    lax.fori_loop(0, 4, finish, 0, unroll=True)

    @pl.when(seq != c)
    def _():
        back_copy(0).wait_send()

    lax.fori_loop(1, GROUP, back_wait, 0)


def on_device(tokens, queries, flags, w_key, w_value, norm_gain):
    count, width = queries.shape[1:]
    dma = pltpu.SemaphoreType.DMA
    any_spec = pl.BlockSpec(memory_space=pltpu.HBM)
    vmem_spec = pl.BlockSpec(memory_space=pltpu.VMEM)
    attended = pl.pallas_call(
        kernel,
        out_shape=jax.ShapeDtypeStruct((count, width), BF16),
        in_specs=[any_spec] * 6,
        out_specs=vmem_spec,
        scratch_shapes=[
            pltpu.VMEM((2, count, tokens.shape[2]), BF16),
            pltpu.VMEM((count, width), BF16),
            pltpu.VMEM((2, 1, count), jnp.int32),
            pltpu.VMEM((1, width), F32),
            pltpu.VMEM((2, 2, 8, width), BF16),
            pltpu.VMEM((2, NX, NZ, NY, 16, 2 * HEAD), BF16),
            pltpu.VMEM((2, 2 * count, 2 * HEAD), F32),
            pltpu.VMEM((2, 4, 2, count, HEAD), BF16),
            pltpu.VMEM((2, HEAD, HEAD), F32),
            pltpu.VMEM((NX, NZ, 8, HEAD), F32),
            pltpu.VMEM((GROUP, HEAD // 4, HEAD), BF16),
            pltpu.VMEM((GROUP, HEAD // 4, HEAD), BF16),
            pltpu.VMEM((GROUP, HEAD // 4, HEAD), BF16),
            pltpu.VMEM((4, 4, HEAD // 4, HEAD), BF16),
            pltpu.VMEM((4, count, HEAD), F32),
            dma((6,)),
            dma((4,)),
            dma((4,)),
            dma((3,)),
            dma((3,)),
            dma((4, 4)),
            dma((4, 4)),
            dma((10,)),
            dma((10,)),
            dma((4, 2, 4)),
            dma((4, 2, 4)),
            dma((4, 2, 4)),
            dma((4, 2, 4)),
            dma((GROUP,)),
            dma((GROUP,)),
            dma((GROUP,)),
            dma((GROUP,)),
        ],
        compiler_params=pltpu.CompilerParams(
            collective_id=0, has_side_effects=True, vmem_limit_bytes=62 << 20
        ),
        name="attention",
    )(tokens[0], queries[0], flags, w_key, w_value, norm_gain.reshape(1, width))
    return attended.reshape(1, count, width)


def solution(mesh):
    in_specs = (
        P("fsdp", "ctx", None),
        P("fsdp", "ctx", None),
        P("fsdp", "ctx"),
        P(("ctx", "fsdp"), None),
        P(("ctx", "fsdp"), None),
        P(),
    )
    out_specs = P("fsdp", "ctx", None)
    return jax.shard_map(
        on_device, mesh=mesh, in_specs=in_specs, out_specs=out_specs, check_vma=False
    )
```

```python
import functools

import jax
import jax.numpy as jnp
from jax import lax
from jax.experimental import pallas as pl
from jax.experimental.pallas import tpu as pltpu
from jax.sharding import PartitionSpec as P

HEAD = 128
MESH = pl.DeviceIdType.MESH
NX, NY, NZ = 4, 4, 16
GROUP = 16
F32, BF16 = jnp.float32, jnp.bfloat16


def device(x, z, y, c):
    return (x * NZ + z, y * 2 + c)


def phi(u):
    return jnp.where(u > 0, u + 1.0, jnp.exp(jnp.minimum(u, 0.0)))


def segments(marks):
    n = marks.shape[1]
    t = lax.broadcasted_iota(jnp.int32, (n, n), 0)
    s = lax.broadcasted_iota(jnp.int32, (n, n), 1)
    wide = jnp.broadcast_to(marks, (n, n)).astype(F32)
    column = jnp.sum(jnp.where(s <= t, wide, 0.0), axis=1, keepdims=True)
    upright = jnp.sum(jnp.where(s == t, wide, 0.0), axis=1, keepdims=True)
    row = jnp.sum(jnp.where(t <= s, jnp.broadcast_to(upright, (n, n)), 0.0), axis=0, keepdims=True)
    last = jnp.sum(marks.astype(F32), axis=1, keepdims=True)
    return column, row, last


def kernel(
    tok, qry, flg, wk, wv, gain, out,
    T, Q, F, G, WB, W, acc, KV, TL, KG, ST, SR, CS, CR, MIX,
    loc, pair_s, pair_r, hop_s, hop_r, z_s, z_r, k_s, k_r, two_s, two_r, three_s, three_r, s1_s, s1_r, s2_s, s2_r,
):
    ctx, fsdp = lax.axis_index("ctx"), lax.axis_index("fsdp")
    x, z = ctx // NZ, lax.rem(ctx, NZ)
    y, c = fsdp // 2, lax.rem(fsdp, 2)
    quad, low = z // 4, lax.rem(z, 4)
    other = 1 - c
    sibling = device(x, z, y, other)

    def at_x(d):
        return device(lax.rem(x + d, NX), z, y, c)

    def at_y(d):
        return device(x, z, lax.rem(y + d, NY), c)

    def at_z(d):
        return device(x, lax.rem(z + d, NZ), y, c)

    def in_quad(d):
        return device(x, quad * 4 + lax.rem(low + d, 4), y, c)

    loads = [
        pltpu.make_async_copy(wk, WB.at[c, 0], loc.at[0]),
        pltpu.make_async_copy(wv, WB.at[c, 1], loc.at[1]),
        pltpu.make_async_copy(flg, F.at[c], loc.at[2]),
        pltpu.make_async_copy(tok, T.at[c], loc.at[3]),
        pltpu.make_async_copy(qry, Q, loc.at[4]),
        pltpu.make_async_copy(gain, G, loc.at[5]),
    ]

    barrier = pltpu.get_barrier_semaphore()

    def greet(to):
        pl.semaphore_signal(barrier, inc=1, device_id=to, device_id_type=MESH)

    def greet_xy(d, carry):
        greet(at_x(d))
        greet(at_y(d))
        greet(in_quad(d))
        return carry

    greet(at_z(4))
    greet(at_z(12))
    lax.fori_loop(1, 4, greet_xy, 0, unroll=True)
    greet(sibling)
    for load in loads:
        load.start()
    for load in loads[:3]:
        load.wait()
    pl.semaphore_wait(barrier, 12)

    def send(src, dst, ss, rs, to):
        return pltpu.make_async_remote_copy(
            src_ref=src, dst_ref=dst, send_sem=ss, recv_sem=rs, device_id=to, device_id_type=MESH
        )

    def same(ref, ss, rs, to):
        return send(ref, ref, ss, rs, to)

    def start(copies):
        for copy in copies:
            copy.start()

    def arrive(copies):
        for copy in copies:
            copy.wait_recv()

    swap_w = same(WB.at[c], pair_s.at[0], pair_r.at[0], sibling)
    swap_f = same(F.at[c], pair_s.at[1], pair_r.at[1], sibling)
    swap_t = same(T.at[c], pair_s.at[2], pair_r.at[2], sibling)
    start([swap_w, swap_f])
    arrive([swap_w])
    both = jnp.concatenate([WB[0].astype(F32), WB[1].astype(F32)], axis=1)
    mine = jnp.where(c == 0, both[:, :, : 2 * HEAD], both[:, :, 2 * HEAD :]).astype(BF16)
    for h in range(2):
        cut = slice(h * HEAD, (h + 1) * HEAD)
        W[h, x, z, y] = jnp.concatenate([mine[0, :, cut], mine[1, :, cut]], axis=1)

    def four(r):
        return pl.ds(lax.rem(quad + r, 4) * 4, 4)

    def hop(d, ahead, k):
        piece = W.at[:, x, lax.rem(z + ahead, NZ), y]
        return same(piece, hop_s.at[k], hop_r.at[k], at_z(d))

    hops = [hop(4, 0, 0), hop(12, 0, 1), hop(12, 4, 2)]

    def share(r):
        piece = W.at[:, x, lax.rem(z + 4 * r, NZ), y]
        return [same(piece, z_s.at[r, d], z_r.at[r, d], in_quad(d)) for d in range(1, 4)]

    def two(r):
        a, b = W.at[0, x, four(r), y], W.at[1, x, four(r), y]
        return [same(a, two_s.at[r, 0, d], two_r.at[r, 0, d], at_y(d)) for d in (1, 3, 2)] + [
            same(b, two_s.at[r, 1, d], two_r.at[r, 1, d], at_x(d)) for d in (1, 3, 2)
        ]

    def three(r):
        a, b = W.at[0, x, four(r)], W.at[1, :, four(r), y]
        return [same(a, three_s.at[r, 0, d], three_r.at[r, 0, d], at_x(d)) for d in (1, 3)] + [
            same(b, three_s.at[r, 1, d], three_r.at[r, 1, d], at_y(d)) for d in (1, 3)
        ]

    def far(r):
        copies = []
        for side, (to, back) in enumerate(((1, 3), (3, 1))):
            part = pl.ds(lax.rem(quad + r, 4) * 4 + 2 * side, 2)
            a = W.at[0, lax.rem(x + back, NX), part]
            b = W.at[1, :, part, lax.rem(y + back, NY)]
            k = 2 - 2 * side
            copies += [
                same(a, three_s.at[r, 0, k], three_r.at[r, 0, k], at_x(to)),
                same(b, three_s.at[r, 1, k], three_r.at[r, 1, k], at_y(to)),
            ]
        return copies

    depth = 4 * NY * 16

    def project(h, part, r):
        q = lax.rem(quad + r, 4)
        cols = pl.ds(pl.multiple_of((part * 4 + q) * depth, depth), depth)
        rows = T[:, :, cols].reshape(2 * HEAD, depth)
        acc[h] += jnp.dot(
            rows, W[h, part, four(r)].reshape(depth, 2 * HEAD), preferred_element_type=F32
        )

    def near_a(r):
        q = lax.rem(quad + r, 4)
        parts = [lax.rem(x + 3 + i, NX) for i in range(3)]
        rows = jnp.concatenate(
            [T[:, :, pl.ds(pl.multiple_of((i * 4 + q) * depth, depth), depth)] for i in parts], axis=2
        )
        sides = jnp.concatenate([W[0, i, four(r)].reshape(depth, 2 * HEAD) for i in parts], axis=0)
        acc[0] += jnp.dot(rows.reshape(2 * HEAD, 3 * depth), sides, preferred_element_type=F32)

    def rest(r):
        project(0, lax.rem(x + 2, NX), r)
        q = lax.rem(quad + r, 4)
        rows = jnp.concatenate(
            [T[:, :, pl.ds(pl.multiple_of((i * 4 + q) * depth, depth), depth)] for i in range(NX)], axis=2
        )
        acc[1] += jnp.dot(
            rows.reshape(2 * HEAD, NX * depth),
            W[1, :, four(r)].reshape(NX * depth, 2 * HEAD),
            preferred_element_type=F32,
        )

    place = lax.rem(z + NZ // 2, GROUP)
    base = lax.rem(x + NX - jnp.where(place < GROUP // 2, 0, 1), NX)

    def member_x(p):
        return lax.rem(base + p // (GROUP // 2), NX)

    def member_z(p):
        return lax.rem(p + NZ // 2, NZ)

    def member(p, core):
        return device(member_x(p), member_z(p), y, core)

    def keep_four(r):
        return KG.at[x, four(r)]

    keep_in = [same(KG.at[x, z], k_s.at[d], k_r.at[d], in_quad(d)) for d in range(1, 4)]
    keep_z = [
        same(keep_four(0), k_s.at[4], k_r.at[4], at_z(4)),
        same(keep_four(0), k_s.at[5], k_r.at[5], at_z(12)),
    ]
    keep_far = [same(keep_four(1), k_s.at[6], k_r.at[6], at_z(12))]
    keep_x = [same(KG.at[x], k_s.at[6 + d], k_r.at[6 + d], at_x(d)) for d in (1, 3)]
    keep_all = keep_in + keep_z + keep_far + keep_x

    start(hops[:2])
    start(share(0))
    loads[3].wait()
    start([swap_t])
    arrive([swap_f])
    column, row, last = [], [], []
    for s in range(2):
        a, b, l = segments(F[s])
        column.append(a)
        row.append(b)
        last.append(l)
    keeps = [jnp.broadcast_to(jnp.where(l > 0, 0.0, 1.0), (4, HEAD)) for l in last]
    KG[x, z] = jnp.concatenate(keeps, axis=0)
    start(keep_in)
    acc[...] = jnp.zeros_like(acc)

    arrive(share(0))
    start(two(0))
    arrive([hops[1]])
    start(hops[2:])
    start(share(1))
    arrive([hops[0]])
    start(share(3))
    arrive(two(0))
    start(three(0))
    arrive(keep_in)
    start(keep_z)
    arrive(hops[2:])
    start(share(2))
    arrive(share(1))
    start(two(1))
    arrive(share(3))
    start(two(3))
    near, ahead = three(0), far(0)
    arrive([near[0], near[2]])
    start(ahead[:2])
    arrive([near[1], near[3]])
    start(ahead[2:])
    arrive(share(2))
    start(two(2))
    arrive(keep_z)
    start(keep_far)
    arrive(two(1))
    start(three(1))
    arrive(two(3))
    start(three(3))
    arrive([swap_t])
    near_a(0)
    arrive(far(0))
    rest(0)
    arrive(two(2))
    start(three(2))
    near, ahead = three(1), far(1)
    arrive([near[0], near[2]])
    start(ahead[:2])
    arrive([near[1], near[3]])
    start(ahead[2:])
    near, ahead = three(3), far(3)
    arrive([near[0], near[2]])
    start(ahead[:2])
    arrive([near[1], near[3]])
    start(ahead[2:])
    arrive(keep_far)
    start(keep_x)
    near, ahead = three(2), far(2)
    arrive([near[0], near[2]])
    start(ahead[:2])
    arrive([near[1], near[3]])
    start(ahead[2:])
    near_a(1)
    near_a(3)
    arrive(far(1))
    rest(1)
    arrive(far(3))
    rest(3)
    near_a(2)
    arrive(far(2))
    rest(2)

    def distant(i):
        step = (i + 1) // 2
        return jnp.where(lax.rem(i, 2) == 1, GROUP // 2 - step, GROUP // 2 + step)

    def one_copy(d):
        p = lax.rem(place + d, GROUP)
        return send(ST.at[p], SR.at[place], s1_s.at[d], s1_r.at[d], member(p, c))

    def one_start(d, carry):
        one_copy(distant(d)).start()
        return carry

    def one_wait(d, carry):
        one_copy(d).wait()
        return carry

    for s in range(2):
        TL[s] = jnp.broadcast_to((column[s] == last[s]).astype(F32), (HEAD, HEAD))

    def states(i, carry):
        s, h = i // 2, lax.rem(i, 2)
        part = acc[h, pl.ds(pl.multiple_of(s * HEAD, HEAD), HEAD), :]
        key = phi(part[:, :HEAD]).astype(BF16)
        value = part[:, HEAD:].astype(BF16)
        KV[s, 2 * c + h, 0] = key
        KV[s, 2 * c + h, 1] = value
        masked = (key.astype(F32) * TL[s]).astype(BF16)
        state = lax.dot_general(masked, value, (((0,), (0,)), ((), ())), preferred_element_type=F32)
        ST[pl.ds(4 * i, 4)] = state.astype(BF16).reshape(4, HEAD // 4, HEAD)
        return carry

    lax.fori_loop(0, 4, states, 0, unroll=True)
    lax.fori_loop(0, GROUP - 1, one_start, 0, unroll=True)
    SR[place] = ST[place]
    swap_kv = same(KV.at[other, pl.ds(2 * c, 2)], pair_s.at[3], pair_r.at[3], sibling)
    start([swap_kv])

    loads[4].wait()
    loads[5].wait()
    my_column = jnp.where(c == 0, column[0], column[1])
    my_row = jnp.where(c == 0, row[0], row[1])
    t = lax.broadcasted_iota(jnp.int32, (HEAD, HEAD), 0)
    u = lax.broadcasted_iota(jnp.int32, (HEAD, HEAD), 1)
    allowed = (u <= t) & (my_column == my_row)
    Q[...] = phi(Q[...].astype(F32)).astype(BF16)
    arrive([swap_kv])
    mask = allowed.astype(F32)

    def inside(h, carry):
        query = Q[:, pl.ds(pl.multiple_of(h * HEAD, HEAD), HEAD)]
        key, value = KV[c, h, 0], KV[c, h, 1]
        scores = lax.dot_general(query, key, (((1,), (1,)), ((), ())), preferred_element_type=F32)
        scores = (scores * mask).astype(BF16)
        MIX[h] = jnp.dot(scores, value, preferred_element_type=F32)
        return carry

    lax.fori_loop(0, 4, inside, 0, unroll=True)
    lax.fori_loop(1, GROUP, one_wait, 0)
    arrive(keep_x)
    seq = place // (GROUP // 2)

    def prefix(b, carried):
        CS[b] = carried.astype(BF16)
        tile = KG[member_x(b), member_z(b)]
        keep = jnp.where(seq == 0, tile[0:1], tile[4:5])
        return keep * carried + SR[b].astype(F32)

    lax.fori_loop(0, GROUP, prefix, jnp.zeros((HEAD // 4, HEAD), F32), unroll=True)

    mine_at = lax.rem(place, GROUP // 2)
    target = CR.at[2 * c + mine_at // 4, lax.rem(mine_at, 4)]
    index = c * 8 + mine_at

    def back_copy(d):
        p = lax.rem(place + d, GROUP)
        return send(CS.at[p], target, s2_s.at[d], s2_r.at[index], member(p, seq))

    def back_start(d, carry):
        back_copy(distant(d)).start()
        return carry

    def back_wait(d, carry):
        back_copy(d).wait_send()
        return carry

    own = pltpu.make_async_copy(CS.at[place], target, s2_r.at[index])

    lax.fori_loop(0, GROUP - 1, back_start, 0, unroll=True)

    @pl.when(seq == c)
    def _():
        own.start()

    @pl.when(seq != c)
    def _():
        back_copy(0).start()

    def back_arrive(i, carry):
        send(CS.at[0], CR.at[i // 4, lax.rem(i, 4)], s2_s.at[0], s2_r.at[i], sibling).wait_recv()
        return carry

    def drain(r, carry):
        for copy in share(r) + two(r) + three(r) + far(r):
            copy.wait_send()
        return carry

    lax.fori_loop(0, 4, drain, 0)
    for copy in hops + keep_all + [swap_w, swap_f, swap_t, swap_kv]:
        copy.wait_send()
    lax.fori_loop(0, GROUP, back_arrive, 0)
    first = (my_column == 0).astype(F32)

    def finish(h, carry):
        cut = pl.ds(pl.multiple_of(h * HEAD, HEAD), HEAD)
        state = CR[h].reshape(HEAD, HEAD)
        mixed = MIX[h] + first * jnp.dot(Q[:, cut], state, preferred_element_type=F32)
        scale = lax.rsqrt(jnp.mean(mixed * mixed, axis=-1, keepdims=True) + 1e-06)
        out[:, cut] = (mixed * scale * G[:, cut]).astype(BF16)
        return carry

    lax.fori_loop(0, 4, finish, 0, unroll=True)

    @pl.when(seq != c)
    def _():
        back_copy(0).wait_send()

    lax.fori_loop(1, GROUP, back_wait, 0)


def on_device(tokens, queries, flags, w_key, w_value, norm_gain):
    count, width = queries.shape[1:]
    dma = pltpu.SemaphoreType.DMA
    any_spec = pl.BlockSpec(memory_space=pltpu.HBM)
    vmem_spec = pl.BlockSpec(memory_space=pltpu.VMEM)
    attended = pl.pallas_call(
        kernel,
        out_shape=jax.ShapeDtypeStruct((count, width), BF16),
        in_specs=[any_spec] * 6,
        out_specs=vmem_spec,
        scratch_shapes=[
            pltpu.VMEM((2, count, tokens.shape[2]), BF16),
            pltpu.VMEM((count, width), BF16),
            pltpu.VMEM((2, 1, count), jnp.int32),
            pltpu.VMEM((1, width), F32),
            pltpu.VMEM((2, 2, 8, width), BF16),
            pltpu.VMEM((2, NX, NZ, NY, 16, 2 * HEAD), BF16),
            pltpu.VMEM((2, 2 * count, 2 * HEAD), F32),
            pltpu.VMEM((2, 4, 2, count, HEAD), BF16),
            pltpu.VMEM((2, HEAD, HEAD), F32),
            pltpu.VMEM((NX, NZ, 8, HEAD), F32),
            pltpu.VMEM((GROUP, HEAD // 4, HEAD), BF16),
            pltpu.VMEM((GROUP, HEAD // 4, HEAD), BF16),
            pltpu.VMEM((GROUP, HEAD // 4, HEAD), BF16),
            pltpu.VMEM((4, 4, HEAD // 4, HEAD), BF16),
            pltpu.VMEM((4, count, HEAD), F32),
            dma((6,)),
            dma((4,)),
            dma((4,)),
            dma((3,)),
            dma((3,)),
            dma((4, 4)),
            dma((4, 4)),
            dma((10,)),
            dma((10,)),
            dma((4, 2, 4)),
            dma((4, 2, 4)),
            dma((4, 2, 4)),
            dma((4, 2, 4)),
            dma((GROUP,)),
            dma((GROUP,)),
            dma((GROUP,)),
            dma((GROUP,)),
        ],
        compiler_params=pltpu.CompilerParams(
            collective_id=0, has_side_effects=True, vmem_limit_bytes=62 << 20
        ),
        name="attention",
    )(tokens[0], queries[0], flags, w_key, w_value, norm_gain.reshape(1, width))
    return attended.reshape(1, count, width)


def solution(mesh):
    in_specs = (
        P("fsdp", "ctx", None),
        P("fsdp", "ctx", None),
        P("fsdp", "ctx"),
        P(("ctx", "fsdp"), None),
        P(("ctx", "fsdp"), None),
        P(),
    )
    out_specs = P("fsdp", "ctx", None)
    return jax.shard_map(
        on_device, mesh=mesh, in_specs=in_specs, out_specs=out_specs, check_vma=False
    )
```

```python
import functools

import jax
import jax.numpy as jnp
from jax import lax
from jax.experimental import pallas as pl
from jax.experimental.pallas import tpu as pltpu
from jax.sharding import PartitionSpec as P

HEAD = 128
MESH = pl.DeviceIdType.MESH
NX, NY, NZ = 4, 4, 16
GROUP = 16
F32, BF16 = jnp.float32, jnp.bfloat16


def device(x, z, y, c):
    return (x * NZ + z, y * 2 + c)


def phi(u):
    return jnp.where(u > 0, u + 1.0, jnp.exp(jnp.minimum(u, 0.0)))


def segments(marks):
    n = marks.shape[1]
    t = lax.broadcasted_iota(jnp.int32, (n, n), 0)
    s = lax.broadcasted_iota(jnp.int32, (n, n), 1)
    wide = jnp.broadcast_to(marks, (n, n)).astype(F32)
    column = jnp.sum(jnp.where(s <= t, wide, 0.0), axis=1, keepdims=True)
    upright = jnp.sum(jnp.where(s == t, wide, 0.0), axis=1, keepdims=True)
    row = jnp.sum(jnp.where(t <= s, jnp.broadcast_to(upright, (n, n)), 0.0), axis=0, keepdims=True)
    last = jnp.sum(marks.astype(F32), axis=1, keepdims=True)
    return column, row, last


def kernel(
    tok, qry, flg, wk, wv, gain, out,
    T, Q, F, G, WB, W, acc, KV, TL, KG, ST, SR, CS, CR, MIX,
    loc, pair_s, pair_r, hop_s, hop_r, z_s, z_r, k_s, k_r, two_s, two_r, three_s, three_r, s1_s, s1_r, s2_s, s2_r,
):
    ctx, fsdp = lax.axis_index("ctx"), lax.axis_index("fsdp")
    x, z = ctx // NZ, lax.rem(ctx, NZ)
    y, c = fsdp // 2, lax.rem(fsdp, 2)
    quad, low = z // 4, lax.rem(z, 4)
    other = 1 - c
    sibling = device(x, z, y, other)

    def at_x(d):
        return device(lax.rem(x + d, NX), z, y, c)

    def at_y(d):
        return device(x, z, lax.rem(y + d, NY), c)

    def at_z(d):
        return device(x, lax.rem(z + d, NZ), y, c)

    def in_quad(d):
        return device(x, quad * 4 + lax.rem(low + d, 4), y, c)

    loads = [
        pltpu.make_async_copy(wk, WB.at[c, 0], loc.at[0]),
        pltpu.make_async_copy(wv, WB.at[c, 1], loc.at[1]),
        pltpu.make_async_copy(flg, F.at[c], loc.at[2]),
        pltpu.make_async_copy(tok, T.at[c], loc.at[3]),
        pltpu.make_async_copy(qry, Q, loc.at[4]),
        pltpu.make_async_copy(gain, G, loc.at[5]),
    ]

    barrier = pltpu.get_barrier_semaphore()

    def greet(to):
        pl.semaphore_signal(barrier, inc=1, device_id=to, device_id_type=MESH)

    def greet_xy(d, carry):
        greet(at_x(d))
        greet(at_y(d))
        greet(in_quad(d))
        return carry

    greet(at_z(4))
    greet(at_z(12))
    lax.fori_loop(1, 4, greet_xy, 0, unroll=True)
    greet(sibling)
    for load in loads:
        load.start()
    for load in loads[:3]:
        load.wait()
    pl.semaphore_wait(barrier, 12)

    def send(src, dst, ss, rs, to):
        return pltpu.make_async_remote_copy(
            src_ref=src, dst_ref=dst, send_sem=ss, recv_sem=rs, device_id=to, device_id_type=MESH
        )

    def same(ref, ss, rs, to):
        return send(ref, ref, ss, rs, to)

    def start(copies):
        for copy in copies:
            copy.start()

    def arrive(copies):
        for copy in copies:
            copy.wait_recv()

    swap_w = same(WB.at[c], pair_s.at[0], pair_r.at[0], sibling)
    swap_f = same(F.at[c], pair_s.at[1], pair_r.at[1], sibling)
    swap_t = same(T.at[c], pair_s.at[2], pair_r.at[2], sibling)
    start([swap_w, swap_f])
    arrive([swap_w])
    both = jnp.concatenate([WB[0].astype(F32), WB[1].astype(F32)], axis=1)
    mine = jnp.where(c == 0, both[:, :, : 2 * HEAD], both[:, :, 2 * HEAD :]).astype(BF16)
    for h in range(2):
        cut = slice(h * HEAD, (h + 1) * HEAD)
        W[h, x, z, y] = jnp.concatenate([mine[0, :, cut], mine[1, :, cut]], axis=1)

    def four(r):
        return pl.ds(lax.rem(quad + r, 4) * 4, 4)

    def hop(d, ahead, k):
        piece = W.at[:, x, lax.rem(z + ahead, NZ), y]
        return same(piece, hop_s.at[k], hop_r.at[k], at_z(d))

    hops = [hop(4, 0, 0), hop(12, 0, 1), hop(12, 4, 2)]

    def share(r):
        piece = W.at[:, x, lax.rem(z + 4 * r, NZ), y]
        return [same(piece, z_s.at[r, d], z_r.at[r, d], in_quad(d)) for d in range(1, 4)]

    def two(r):
        a, b = W.at[0, x, four(r), y], W.at[1, x, four(r), y]
        return [same(a, two_s.at[r, 0, d], two_r.at[r, 0, d], at_y(d)) for d in (1, 3, 2)] + [
            same(b, two_s.at[r, 1, d], two_r.at[r, 1, d], at_x(d)) for d in (1, 3, 2)
        ]

    def three(r):
        a, b = W.at[0, x, four(r)], W.at[1, :, four(r), y]
        return [same(a, three_s.at[r, 0, d], three_r.at[r, 0, d], at_x(d)) for d in (1, 3)] + [
            same(b, three_s.at[r, 1, d], three_r.at[r, 1, d], at_y(d)) for d in (1, 3)
        ]

    def far(r):
        copies = []
        for side, (to, back) in enumerate(((1, 3), (3, 1))):
            part = pl.ds(lax.rem(quad + r, 4) * 4 + 2 * side, 2)
            a = W.at[0, lax.rem(x + back, NX), part]
            b = W.at[1, :, part, lax.rem(y + back, NY)]
            k = 2 - 2 * side
            copies += [
                same(a, three_s.at[r, 0, k], three_r.at[r, 0, k], at_x(to)),
                same(b, three_s.at[r, 1, k], three_r.at[r, 1, k], at_y(to)),
            ]
        return copies

    depth = 4 * NY * 16

    def project(h, part, r):
        q = lax.rem(quad + r, 4)
        cols = pl.ds(pl.multiple_of((part * 4 + q) * depth, depth), depth)
        rows = T[:, :, cols].reshape(2 * HEAD, depth)
        acc[h] += jnp.dot(
            rows, W[h, part, four(r)].reshape(depth, 2 * HEAD), preferred_element_type=F32
        )

    def near_a(r):
        q = lax.rem(quad + r, 4)
        parts = [lax.rem(x + 3 + i, NX) for i in range(3)]
        rows = jnp.concatenate(
            [T[:, :, pl.ds(pl.multiple_of((i * 4 + q) * depth, depth), depth)] for i in parts], axis=2
        )
        sides = jnp.concatenate([W[0, i, four(r)].reshape(depth, 2 * HEAD) for i in parts], axis=0)
        acc[0] += jnp.dot(rows.reshape(2 * HEAD, 3 * depth), sides, preferred_element_type=F32)

    def rest(r):
        project(0, lax.rem(x + 2, NX), r)
        q = lax.rem(quad + r, 4)
        rows = jnp.concatenate(
            [T[:, :, pl.ds(pl.multiple_of((i * 4 + q) * depth, depth), depth)] for i in range(NX)], axis=2
        )
        acc[1] += jnp.dot(
            rows.reshape(2 * HEAD, NX * depth),
            W[1, :, four(r)].reshape(NX * depth, 2 * HEAD),
            preferred_element_type=F32,
        )

    place = lax.rem(z + NZ // 2, GROUP)
    base = lax.rem(x + NX - jnp.where(place < GROUP // 2, 0, 1), NX)

    def member_x(p):
        return lax.rem(base + p // (GROUP // 2), NX)

    def member_z(p):
        return lax.rem(p + NZ // 2, NZ)

    def member(p, core):
        return device(member_x(p), member_z(p), y, core)

    def keep_four(r):
        return KG.at[x, four(r)]

    keep_in = [same(KG.at[x, z], k_s.at[d], k_r.at[d], in_quad(d)) for d in range(1, 4)]
    keep_z = [
        same(keep_four(0), k_s.at[4], k_r.at[4], at_z(4)),
        same(keep_four(0), k_s.at[5], k_r.at[5], at_z(12)),
    ]
    keep_far = [same(keep_four(1), k_s.at[6], k_r.at[6], at_z(12))]
    keep_x = [same(KG.at[x], k_s.at[6 + d], k_r.at[6 + d], at_x(d)) for d in (1, 3)]
    keep_all = keep_in + keep_z + keep_far + keep_x

    start(hops[:2])
    start(share(0))
    loads[3].wait()
    start([swap_t])
    arrive([swap_f])
    column, row, last = [], [], []
    for s in range(2):
        a, b, l = segments(F[s])
        column.append(a)
        row.append(b)
        last.append(l)
    keeps = [jnp.broadcast_to(jnp.where(l > 0, 0.0, 1.0), (4, HEAD)) for l in last]
    KG[x, z] = jnp.concatenate(keeps, axis=0)
    start(keep_in)
    acc[...] = jnp.zeros_like(acc)

    arrive(share(0))
    start(two(0))
    arrive([hops[1]])
    start(hops[2:])
    start(share(1))
    arrive([hops[0]])
    start(share(3))
    earlier, later = two(0), three(0)
    arrive(earlier[:3])
    start(later[:2])
    arrive(earlier[3:])
    start(later[2:])
    arrive(keep_in)
    start(keep_z)
    arrive(hops[2:])
    start(share(2))
    arrive(share(1))
    start(two(1))
    arrive(share(3))
    start(two(3))
    near, ahead = three(0), far(0)
    arrive([near[0], near[2]])
    start(ahead[:2])
    arrive([near[1], near[3]])
    start(ahead[2:])
    arrive(share(2))
    start(two(2))
    arrive(keep_z)
    start(keep_far)
    earlier, later = two(1), three(1)
    arrive(earlier[:3])
    start(later[:2])
    arrive(earlier[3:])
    start(later[2:])
    earlier, later = two(3), three(3)
    arrive(earlier[:3])
    start(later[:2])
    arrive(earlier[3:])
    start(later[2:])
    arrive([swap_t])
    near_a(0)
    arrive(far(0))
    rest(0)
    earlier, later = two(2), three(2)
    arrive(earlier[:3])
    start(later[:2])
    arrive(earlier[3:])
    start(later[2:])
    near, ahead = three(1), far(1)
    arrive([near[0], near[2]])
    start(ahead[:2])
    arrive([near[1], near[3]])
    start(ahead[2:])
    near, ahead = three(3), far(3)
    arrive([near[0], near[2]])
    start(ahead[:2])
    arrive([near[1], near[3]])
    start(ahead[2:])
    arrive(keep_far)
    start(keep_x)
    near, ahead = three(2), far(2)
    arrive([near[0], near[2]])
    start(ahead[:2])
    arrive([near[1], near[3]])
    start(ahead[2:])
    near_a(1)
    near_a(3)
    arrive(far(1))
    rest(1)
    arrive(far(3))
    rest(3)
    near_a(2)
    arrive(far(2))
    rest(2)

    def distant(i):
        step = (i + 1) // 2
        return jnp.where(lax.rem(i, 2) == 1, GROUP // 2 - step, GROUP // 2 + step)

    def one_copy(d):
        p = lax.rem(place + d, GROUP)
        return send(ST.at[p], SR.at[place], s1_s.at[d], s1_r.at[d], member(p, c))

    def one_start(d, carry):
        one_copy(distant(d)).start()
        return carry

    def one_wait(d, carry):
        one_copy(d).wait()
        return carry

    for s in range(2):
        TL[s] = jnp.broadcast_to((column[s] == last[s]).astype(F32), (HEAD, HEAD))

    def states(i, carry):
        s, h = i // 2, lax.rem(i, 2)
        part = acc[h, pl.ds(pl.multiple_of(s * HEAD, HEAD), HEAD), :]
        key = phi(part[:, :HEAD]).astype(BF16)
        value = part[:, HEAD:].astype(BF16)
        KV[s, 2 * c + h, 0] = key
        KV[s, 2 * c + h, 1] = value
        masked = (key.astype(F32) * TL[s]).astype(BF16)
        state = lax.dot_general(masked, value, (((0,), (0,)), ((), ())), preferred_element_type=F32)
        ST[pl.ds(4 * i, 4)] = state.astype(BF16).reshape(4, HEAD // 4, HEAD)
        return carry

    lax.fori_loop(0, 4, states, 0, unroll=True)
    lax.fori_loop(0, GROUP - 1, one_start, 0, unroll=True)
    SR[place] = ST[place]
    swap_kv = same(KV.at[other, pl.ds(2 * c, 2)], pair_s.at[3], pair_r.at[3], sibling)
    start([swap_kv])

    loads[4].wait()
    loads[5].wait()
    my_column = jnp.where(c == 0, column[0], column[1])
    my_row = jnp.where(c == 0, row[0], row[1])
    t = lax.broadcasted_iota(jnp.int32, (HEAD, HEAD), 0)
    u = lax.broadcasted_iota(jnp.int32, (HEAD, HEAD), 1)
    allowed = (u <= t) & (my_column == my_row)
    Q[...] = phi(Q[...].astype(F32)).astype(BF16)
    arrive([swap_kv])
    mask = allowed.astype(F32)

    def inside(h, carry):
        query = Q[:, pl.ds(pl.multiple_of(h * HEAD, HEAD), HEAD)]
        key, value = KV[c, h, 0], KV[c, h, 1]
        scores = lax.dot_general(query, key, (((1,), (1,)), ((), ())), preferred_element_type=F32)
        scores = (scores * mask).astype(BF16)
        MIX[h] = jnp.dot(scores, value, preferred_element_type=F32)
        return carry

    lax.fori_loop(0, 4, inside, 0, unroll=True)
    lax.fori_loop(1, GROUP, one_wait, 0)
    arrive(keep_x)
    seq = place // (GROUP // 2)

    def prefix(b, carried):
        CS[b] = carried.astype(BF16)
        tile = KG[member_x(b), member_z(b)]
        keep = jnp.where(seq == 0, tile[0:1], tile[4:5])
        return keep * carried + SR[b].astype(F32)

    lax.fori_loop(0, GROUP, prefix, jnp.zeros((HEAD // 4, HEAD), F32), unroll=True)

    mine_at = lax.rem(place, GROUP // 2)
    target = CR.at[2 * c + mine_at // 4, lax.rem(mine_at, 4)]
    index = c * 8 + mine_at

    def back_copy(d):
        p = lax.rem(place + d, GROUP)
        return send(CS.at[p], target, s2_s.at[d], s2_r.at[index], member(p, seq))

    def back_start(d, carry):
        back_copy(distant(d)).start()
        return carry

    def back_wait(d, carry):
        back_copy(d).wait_send()
        return carry

    own = pltpu.make_async_copy(CS.at[place], target, s2_r.at[index])

    lax.fori_loop(0, GROUP - 1, back_start, 0, unroll=True)

    @pl.when(seq == c)
    def _():
        own.start()

    @pl.when(seq != c)
    def _():
        back_copy(0).start()

    def back_arrive(i, carry):
        send(CS.at[0], CR.at[i // 4, lax.rem(i, 4)], s2_s.at[0], s2_r.at[i], sibling).wait_recv()
        return carry

    def drain(r, carry):
        for copy in share(r) + two(r) + three(r) + far(r):
            copy.wait_send()
        return carry

    lax.fori_loop(0, 4, drain, 0)
    for copy in hops + keep_all + [swap_w, swap_f, swap_t, swap_kv]:
        copy.wait_send()
    lax.fori_loop(0, GROUP, back_arrive, 0)
    first = (my_column == 0).astype(F32)

    def finish(h, carry):
        cut = pl.ds(pl.multiple_of(h * HEAD, HEAD), HEAD)
        state = CR[h].reshape(HEAD, HEAD)
        mixed = MIX[h] + first * jnp.dot(Q[:, cut], state, preferred_element_type=F32)
        scale = lax.rsqrt(jnp.mean(mixed * mixed, axis=-1, keepdims=True) + 1e-06)
        out[:, cut] = (mixed * scale * G[:, cut]).astype(BF16)
        return carry

    lax.fori_loop(0, 4, finish, 0, unroll=True)

    @pl.when(seq != c)
    def _():
        back_copy(0).wait_send()

    lax.fori_loop(1, GROUP, back_wait, 0)


def on_device(tokens, queries, flags, w_key, w_value, norm_gain):
    count, width = queries.shape[1:]
    dma = pltpu.SemaphoreType.DMA
    any_spec = pl.BlockSpec(memory_space=pltpu.HBM)
    vmem_spec = pl.BlockSpec(memory_space=pltpu.VMEM)
    attended = pl.pallas_call(
        kernel,
        out_shape=jax.ShapeDtypeStruct((count, width), BF16),
        in_specs=[any_spec] * 6,
        out_specs=vmem_spec,
        scratch_shapes=[
            pltpu.VMEM((2, count, tokens.shape[2]), BF16),
            pltpu.VMEM((count, width), BF16),
            pltpu.VMEM((2, 1, count), jnp.int32),
            pltpu.VMEM((1, width), F32),
            pltpu.VMEM((2, 2, 8, width), BF16),
            pltpu.VMEM((2, NX, NZ, NY, 16, 2 * HEAD), BF16),
            pltpu.VMEM((2, 2 * count, 2 * HEAD), F32),
            pltpu.VMEM((2, 4, 2, count, HEAD), BF16),
            pltpu.VMEM((2, HEAD, HEAD), F32),
            pltpu.VMEM((NX, NZ, 8, HEAD), F32),
            pltpu.VMEM((GROUP, HEAD // 4, HEAD), BF16),
            pltpu.VMEM((GROUP, HEAD // 4, HEAD), BF16),
            pltpu.VMEM((GROUP, HEAD // 4, HEAD), BF16),
            pltpu.VMEM((4, 4, HEAD // 4, HEAD), BF16),
            pltpu.VMEM((4, count, HEAD), F32),
            dma((6,)),
            dma((4,)),
            dma((4,)),
            dma((3,)),
            dma((3,)),
            dma((4, 4)),
            dma((4, 4)),
            dma((10,)),
            dma((10,)),
            dma((4, 2, 4)),
            dma((4, 2, 4)),
            dma((4, 2, 4)),
            dma((4, 2, 4)),
            dma((GROUP,)),
            dma((GROUP,)),
            dma((GROUP,)),
            dma((GROUP,)),
        ],
        compiler_params=pltpu.CompilerParams(
            collective_id=0, has_side_effects=True, vmem_limit_bytes=62 << 20
        ),
        name="attention",
    )(tokens[0], queries[0], flags, w_key, w_value, norm_gain.reshape(1, width))
    return attended.reshape(1, count, width)


def solution(mesh):
    in_specs = (
        P("fsdp", "ctx", None),
        P("fsdp", "ctx", None),
        P("fsdp", "ctx"),
        P(("ctx", "fsdp"), None),
        P(("ctx", "fsdp"), None),
        P(),
    )
    out_specs = P("fsdp", "ctx", None)
    return jax.shard_map(
        on_device, mesh=mesh, in_specs=in_specs, out_specs=out_specs, check_vma=False
    )
```
